32 devices in a mesh: rows: 8 (over z, y), cols: 4 (over x, core).
Axes of the slice: x: 2, y: 2, z: 4, core: 2. Of those that a mesh axis runs over, the one named last changes fastest.
Arguments:
- tokens: bfloat16 [8192, 2048], P('rows', 'cols'), may hold values from -6 to 6
- gain_attn: bfloat16 [2048], P('cols'), may hold values from -0.5 to 0.5
- gain_mlp: bfloat16 [2048], P('cols'), may hold values from -0.5 to 0.5
- w_q: bfloat16 [2048, 2048], P('rows', 'cols'), may hold values from -0.125 to 0.125
- w_kv: bfloat16 [2048, 512], P('rows', 'cols'), may hold values from -0.125 to 0.125
- a_qkv: bfloat16 [2048, 256], P('rows'), may hold values from -0.125 to 0.125
- b_q: bfloat16 [256, 2048], P('rows', 'cols'), may hold values from -0.1875 to 0.1875
- b_kv: bfloat16 [256, 512], P('rows', 'cols'), may hold values from -0.1875 to 0.1875
- w_o: bfloat16 [2048, 2048], P('cols', 'rows'), may hold values from -1.5 to 1.5
- a_o: bfloat16 [2048, 256], P('cols', 'rows'), may hold values from -1.5 to 1.5
- b_o: bfloat16 [256, 2048], P('rows', 'cols'), may hold values from -0.1875 to 0.1875
- w_gate: bfloat16 [2048, 16384], P('rows', 'cols'), may hold values from -0.125 to 0.125
- w_up: bfloat16 [2048, 16384], P('rows', 'cols'), may hold values from -0.125 to 0.125
- a_gu: bfloat16 [2048, 256], P('rows'), may hold values from -0.125 to 0.125
- b_gate: bfloat16 [256, 16384], P('rows', 'cols'), may hold values from -0.1875 to 0.1875
- b_up: bfloat16 [256, 16384], P('rows', 'cols'), may hold values from -0.1875 to 0.1875
- w_down: bfloat16 [16384, 2048], P('cols', 'rows'), may hold values from -0.09375 to 0.09375
- a_down: bfloat16 [16384, 256], P('cols', 'rows'), may hold values from -0.09375 to 0.09375
- b_down: bfloat16 [256, 2048], P('rows', 'cols'), may hold values from -0.1875 to 0.1875
- lengths: int32 [8], replicated, may hold values from 256 to 1024, as said below
- teacher: bfloat16 [8192, 2048], P('rows', 'cols'), may hold values from -6 to 6
- out_grad: bfloat16 [8192, 2048], P('rows', 'cols'), may hold values from -6 to 6
Outputs:
- output: bfloat16 [8192, 2048], P('rows', 'cols')
- loss: float32 [1], replicated
- grad_tokens: float32 [8192, 2048], P('rows', 'cols')
- grad_gain_attn: float32 [2048], P('cols')
- grad_gain_mlp: float32 [2048], P('cols')
- grad_w_q: float32 [2048, 2048], P('rows', 'cols')
- grad_w_kv: float32 [2048, 512], P('rows', 'cols')
- grad_a_qkv: float32 [2048, 256], P('rows')
- grad_b_q: float32 [256, 2048], P('rows', 'cols')
- grad_b_kv: float32 [256, 512], P('rows', 'cols')
- grad_w_o: float32 [2048, 2048], P('cols', 'rows')
- grad_a_o: float32 [2048, 256], P('cols', 'rows')
- grad_b_o: float32 [256, 2048], P('rows', 'cols')
- grad_w_gate: float32 [2048, 16384], P('rows', 'cols')
- grad_w_up: float32 [2048, 16384], P('rows', 'cols')
- grad_a_gu: float32 [2048, 256], P('rows')
- grad_b_gate: float32 [256, 16384], P('rows', 'cols')
- grad_b_up: float32 [256, 16384], P('rows', 'cols')
- grad_w_down: float32 [16384, 2048], P('cols', 'rows')
- grad_a_down: float32 [16384, 256], P('cols', 'rows')
- grad_b_down: float32 [256, 2048], P('rows', 'cols')
The draws below stay inside these ranges and needn't reach their ends.
Inputs may be any that keep to these rules, and one draw needn't show every extreme that they name: `lengths`: each sequence's valid tokens stand at its start; some sequence is valid in all 1024 slots.
All inputs are finite; a program needn't handle non-finite values.
Results may differ from the reference program's by a relative error of at most 0.02.
Values may be sent and summed in bfloat16 or wider, within the bound.
No kernel may reach another device: no remote copies, remote signals or barrier semaphores. Data moves between devices by JAX's collectives and lax.ppermute only.
A program may use at most 320 MiB of HBM per device.

```python
import jax
import jax.numpy as jnp
from jax import lax

D = 2048
FF = 16384
HD = 256
R = 256
LEN = 1024
HQ = 2048
SEQS = 8
TOKENS = 8192


def draw_lengths(key, part):
    first_key = jax.random.fold_in(key, 11)
    second_key = jax.random.fold_in(key, 12)
    drawn = jax.random.randint(first_key, (SEQS,), LEN // 4, LEN + 1)
    chosen = jax.random.randint(second_key, (), 0, SEQS)
    return jnp.where(jnp.arange(SEQS) == chosen, LEN, drawn).astype(jnp.int32)


def level_of(rng, shape, cuts, low, top_value):
    gain = 1.0
    for axis_at, shards_of in cuts:
        draws = jax.random.uniform(jax.random.fold_in(jax.random.fold_in(rng, 6), axis_at), (shards_of,), jnp.float32, low / len(cuts), top_value / len(cuts))
        gain = gain * jnp.repeat(jnp.exp(draws), shape[axis_at] // shards_of).reshape((-1,) + (1,) * (len(shape) - 1 - axis_at))
    return gain


def gaussian(key, extent, width, reach, cuts=(), kind=jnp.bfloat16):
    level = level_of(key, extent, cuts, -0.22, 0.18) if cuts else 1.0
    entries = jax.random.normal(key, extent, jnp.float32) * width * level
    return jnp.minimum(jnp.maximum(entries, -reach), reach).astype(kind)


def setup_inputs(seed: int = 0) -> dict:
    seeds = jax.random.split(jax.random.key(seed), 23)
    tokens = gaussian(seeds[0], (TOKENS, D), 1.0, 6.0, ((0, 8), (1, 4)))
    gain_attn = jnp.clip(jax.random.uniform(seeds[1], (D,), jnp.float32, -0.5, 0.5) * level_of(seeds[1], (D,), ((0, 4),), -0.4, 0.0), -0.5, 0.5).astype(jnp.bfloat16)
    gain_mlp = jnp.clip(jax.random.uniform(seeds[2], (D,), jnp.float32, -0.5, 0.5) * level_of(seeds[2], (D,), ((0, 4),), -0.4, 0.0), -0.5, 0.5).astype(jnp.bfloat16)
    w_q = gaussian(seeds[3], (D, HQ), D ** -0.5, 0.125, ((0, 8), (1, 4)))
    w_kv = gaussian(seeds[4], (D, 2 * HD), D ** -0.5, 0.125, ((0, 8), (1, 4)))
    a_qkv = gaussian(seeds[5], (D, R), D ** -0.5, 0.125, ((0, 8),))
    b_q = gaussian(seeds[6], (R, HQ), (4 * R) ** -0.5, 0.1875, ((0, 8), (1, 4)))
    b_kv = gaussian(seeds[7], (R, 2 * HD), (4 * R) ** -0.5, 0.1875, ((0, 8), (1, 4)))
    w_o = gaussian(seeds[8], (HQ, D), (HQ // 128) ** -0.5, 1.5, ((0, 4), (1, 8)))
    a_o = gaussian(seeds[9], (HQ, R), (HQ // 128) ** -0.5, 1.5, ((0, 4), (1, 8)))
    b_o = gaussian(seeds[10], (R, D), (4 * R) ** -0.5, 0.1875, ((0, 8), (1, 4)))
    w_gate = gaussian(seeds[11], (D, FF), D ** -0.5, 0.125, ((0, 8), (1, 4)))
    w_up = gaussian(seeds[12], (D, FF), D ** -0.5, 0.125, ((0, 8), (1, 4)))
    a_gu = gaussian(seeds[13], (D, R), D ** -0.5, 0.125, ((0, 8),))
    b_gate = gaussian(seeds[14], (R, FF), (4 * R) ** -0.5, 0.1875, ((0, 8), (1, 4)))
    b_up = gaussian(seeds[15], (R, FF), (4 * R) ** -0.5, 0.1875, ((0, 8), (1, 4)))
    w_down = gaussian(seeds[16], (FF, D), (FF // 4) ** -0.5, 0.09375, ((0, 4), (1, 8)))
    a_down = gaussian(seeds[17], (FF, R), (FF // 4) ** -0.5, 0.09375, ((0, 4), (1, 8)))
    b_down = gaussian(seeds[18], (R, D), (4 * R) ** -0.5, 0.1875, ((0, 8), (1, 4)))
    lengths = draw_lengths(jax.random.fold_in(seeds[22], 71), 0)
    teacher = gaussian(seeds[20], (TOKENS, D), 1.0, 6.0, ((0, 8), (1, 4)))
    out_grad = gaussian(seeds[21], (TOKENS, D), 1.0, 6.0, ((0, 8), (1, 4)))
    return {"tokens": tokens, "gain_attn": gain_attn, "gain_mlp": gain_mlp, "w_q": w_q, "w_kv": w_kv, "a_qkv": a_qkv, "b_q": b_q, "b_kv": b_kv, "w_o": w_o, "a_o": a_o, "b_o": b_o, "w_gate": w_gate, "w_up": w_up, "a_gu": a_gu, "b_gate": b_gate, "b_up": b_up, "w_down": w_down, "a_down": a_down, "b_down": b_down, "lengths": lengths, "teacher": teacher, "out_grad": out_grad}


@jax.custom_vjp
def low(v):
    return lax.optimization_barrier(v.astype(jnp.bfloat16)).astype(jnp.float32)

@jax.custom_vjp
def low_back(v):
    return v

def low_keep(v):
    return (low(v), None)

def low_pass(kept, grad):
    return (grad,)

def back_keep(v):
    return (v, None)

def back_low(kept, grad):
    return (low(grad),)
low.defvjp(low_keep, low_pass)
low_back.defvjp(back_keep, back_low)

def matmul_full(former, latter):
    return jnp.dot(former, latter, precision=lax.Precision.HIGHEST, preferred_element_type=jnp.float32)

def root_norm(values_in, gain_row):
    mean_square = lax.optimization_barrier(jnp.mean(values_in * values_in, axis=-1, keepdims=True))
    return values_in * lax.rsqrt(mean_square + 1e-06) * (1.0 + gain_row)

def angles(length, head_size):
    half_size = head_size // 2
    inverse = 10000.0 ** (-(jnp.arange(half_size, dtype=jnp.float32) * 2.0 / head_size))
    theta = jnp.arange(length, dtype=jnp.float32)[:, None] * inverse[None, :]
    return (jnp.cos(theta), jnp.sin(theta))

def rotate(values_in, cosine_table, sine_table):
    half_size = values_in.shape[-1] // 2
    first_half = values_in[..., :half_size]
    second_half = values_in[..., half_size:]
    return jnp.concatenate([first_half * cosine_table - second_half * sine_table, second_half * cosine_table + first_half * sine_table], axis=-1)

def attend_one(packed):
    query_rows, key_rows, value_rows, length = packed
    key_count = key_rows.shape[0]
    scores = low_back(jnp.einsum('hqd,kd->hqk', query_rows, key_rows, precision=lax.Precision.HIGHEST))
    row_place = jnp.arange(key_count)[:, None]
    col_place = jnp.arange(key_count)[None, :]
    allowed = ((col_place <= row_place) & (col_place < length))[None]
    probability = low(jax.nn.softmax(jnp.where(allowed, scores, -1e+30), axis=-1))
    return low_back(low(jnp.einsum('hqk,kd->hqd', probability, value_rows, precision=lax.Precision.HIGHEST)))

def layer_group(params, packed):
    gain_attn, gain_mlp, w_q, w_kv, a_qkv, b_q, b_kv, w_o, a_o, b_o, w_gate, w_up, a_gu, b_gate, b_up, w_down, a_down, b_down = params
    block_rows, block_lengths = packed
    group_size = block_lengths.shape[0]
    row_count = block_rows.shape[0]
    length = row_count // group_size
    head_size = b_kv.shape[1] // 2
    head_count = w_q.shape[1] // head_size
    normed = low(root_norm(block_rows, gain_attn))
    lowrank = low_back(low(matmul_full(normed, a_qkv)))
    q_lin = low_back(matmul_full(normed, w_q) + matmul_full(lowrank, b_q))
    kv_lin = low_back(matmul_full(normed, w_kv) + matmul_full(lowrank, b_kv))
    cosine_table, sine_table = angles(length, head_size)
    queries = q_lin.reshape(group_size, length, head_count, head_size).transpose(0, 2, 1, 3)
    queries = low(rotate(queries, cosine_table, sine_table) * head_size ** (-0.5))
    keys = low(rotate(kv_lin[:, :head_size].reshape(group_size, length, head_size), cosine_table, sine_table))
    values = low(kv_lin[:, head_size:].reshape(group_size, length, head_size))
    attended = lax.map(jax.checkpoint(attend_one), (queries, keys, values, block_lengths))
    attended = attended.transpose(0, 2, 1, 3).reshape(row_count, head_count * head_size)
    low_o = low_back(low(matmul_full(attended, a_o)))
    branch_one = low_back(matmul_full(attended, w_o) + matmul_full(low_o, b_o))
    middle = block_rows + branch_one
    normed_two = low(root_norm(low(middle), gain_mlp))
    low_g = low_back(low(matmul_full(normed_two, a_gu)))
    gate_lin = low_back(matmul_full(normed_two, w_gate) + matmul_full(low_g, b_gate))
    up_lin = low_back(matmul_full(normed_two, w_up) + matmul_full(low_g, b_up))
    hidden = low(jax.nn.gelu(gate_lin, approximate=True) * up_lin)
    low_d = low_back(low(matmul_full(hidden, a_down)))
    branch_two = low_back(matmul_full(hidden, w_down) + matmul_full(low_d, b_down))
    return middle + branch_two

def reference(tokens, gain_attn, gain_mlp, w_q, w_kv, a_qkv, b_q, b_kv, w_o, a_o, b_o, w_gate, w_up, a_gu, b_gate, b_up, w_down, a_down, b_down, lengths, teacher, out_grad):
    params = tuple((weight_in.astype(jnp.float32) for weight_in in (gain_attn, gain_mlp, w_q, w_kv, a_qkv, b_q, b_kv, w_o, a_o, b_o, w_gate, w_up, a_gu, b_gate, b_up, w_down, a_down, b_down)))
    seq_count = lengths.shape[0]
    group_size = 4 if seq_count % 4 == 0 else 2 if seq_count % 2 == 0 else 1
    inputs = tokens.astype(jnp.float32)
    features = inputs.shape[1]

    def forward(inputs_in, params_in):
        blocks = inputs_in.reshape(seq_count // group_size, group_size * LEN, features)
        block_lengths = lengths.reshape(seq_count // group_size, group_size)
        block_step = jax.checkpoint(lambda packed: layer_group(params_in, packed))
        outputs = lax.map(block_step, (blocks, block_lengths))
        return outputs.reshape(inputs_in.shape)
    result, pullback = jax.vjp(forward, inputs, params)
    positions = jnp.arange(LEN)
    valid_rows = (positions[None, :] < lengths[:, None]).reshape(-1, 1).astype(jnp.float32)
    valid_count = jnp.sum(lengths).astype(jnp.float32)
    error_rows = result - teacher.astype(jnp.float32)
    loss_value = jnp.sum(error_rows * error_rows * valid_rows) / (2.0 * valid_count)
    seed_grad = out_grad.astype(jnp.float32) + result.shape[0] / valid_count * error_rows * valid_rows
    grad_inputs, grads = pullback(seed_grad)
    return (result.astype(jnp.bfloat16), loss_value.reshape(1), grad_inputs, grads[0], grads[1], grads[2], grads[3], grads[4], grads[5], grads[6], grads[7], grads[8], grads[9], grads[10], grads[11], grads[12], grads[13], grads[14], grads[15], grads[16], grads[17])
```

```python
import jax
import jax.numpy as jnp
from jax import lax
from jax.sharding import PartitionSpec as P

NORM_EPS = 1e-06
BF = jnp.bfloat16
F32 = jnp.float32


def product(former, latter):
    return jnp.dot(former, latter, preferred_element_type=F32)


def left_trans(former, latter):
    return lax.dot_general(
        former, latter, (((0,), (0,)), ((), ())), preferred_element_type=F32
    )


def right_trans(former, latter):
    return lax.dot_general(
        former, latter, (((1,), (1,)), ((), ())), preferred_element_type=F32
    )


def angles(length, head_size):
    half_size = head_size // 2
    inverse = 10000.0 ** (-(jnp.arange(half_size, dtype=F32) * 2.0 / head_size))
    theta = jnp.arange(length, dtype=F32)[:, None] * inverse[None, :]
    return (jnp.cos(theta), jnp.sin(theta))


def rotate(values_in, cosine_table, sine_table):
    half_size = values_in.shape[-1] // 2
    first_half = values_in[..., :half_size]
    second_half = values_in[..., half_size:]
    return jnp.concatenate(
        [
            first_half * cosine_table - second_half * sine_table,
            second_half * cosine_table + first_half * sine_table,
        ],
        axis=-1,
    )


def allowed_mask(key_count, length):
    row_place = jnp.arange(key_count)[:, None]
    col_place = jnp.arange(key_count)[None, :]
    return ((col_place <= row_place) & (col_place < length))[None]


def attend_forward(query_rows, key_rows, value_rows, length):
    allowed = allowed_mask(key_rows.shape[0], length)
    scores = jnp.einsum("hqd,kd->hqk", query_rows, key_rows, preferred_element_type=F32)
    masked = jnp.where(allowed, scores, -1e30)
    largest = jnp.max(masked, axis=-1, keepdims=True)
    exponent = jnp.exp(masked - largest)
    totals = jnp.sum(exponent, axis=-1, keepdims=True)
    probability = (exponent / totals).astype(BF)
    attended = jnp.einsum("hqk,kd->hqd", probability, value_rows, preferred_element_type=F32)
    return (attended.astype(BF), (largest + jnp.log(totals))[..., 0])


def attend_backward(query_rows, key_rows, value_rows, length, log_total, grad_out):
    allowed = allowed_mask(key_rows.shape[0], length)
    scores = jnp.einsum("hqd,kd->hqk", query_rows, key_rows, preferred_element_type=F32)
    probability = jnp.where(allowed, jnp.exp(scores - log_total[..., None]), 0.0)
    grad_prob = jnp.einsum("hqd,kd->hqk", grad_out, value_rows, preferred_element_type=F32)
    row_terms = jnp.sum(probability * grad_prob, axis=-1, keepdims=True)
    grad_scores = (probability * (grad_prob - row_terms)).astype(BF)
    grad_query = jnp.einsum("hqk,kd->hqd", grad_scores, key_rows, preferred_element_type=F32)
    grad_key = jnp.einsum("hqk,hqd->kd", grad_scores, query_rows, preferred_element_type=F32)
    grad_value = jnp.einsum(
        "hqk,hqd->kd", probability.astype(BF), grad_out, preferred_element_type=F32
    )
    return (grad_query, grad_key, grad_value)


def norm_scale(values_in):
    return lax.rsqrt(jnp.mean(values_in * values_in, axis=-1, keepdims=True) + NORM_EPS)


def norm_forward(values_in, gain_row):
    row_scale = norm_scale(values_in)
    return ((values_in * row_scale * (1.0 + gain_row)).astype(BF), row_scale)


def norm_backward(grad_rows, rows_in, gain_row, row_scale):
    factor = 1.0 + gain_row
    row_dots = jnp.sum(grad_rows * factor * rows_in, axis=-1, keepdims=True)
    grad_input = (
        row_scale * factor * grad_rows
        - rows_in * (row_scale * row_scale * row_scale) * row_dots / rows_in.shape[1]
    )
    return (grad_input, jnp.sum(grad_rows * rows_in * row_scale, axis=0))


def geglu(gate_lin, up_lin):
    return jax.nn.gelu(gate_lin, approximate=True) * up_lin


def solution(mesh):
    row_devices = mesh.shape["rows"]
    col_devices = mesh.shape["cols"]
    nk = 2
    nx = col_devices // nk
    nz = 4 if row_devices % 4 == 0 else row_devices
    ny = row_devices // nz
    BOTH = ("rows", "cols")

    def permute(value, move):
        pairs = []
        for z in range(nz):
            for y in range(ny):
                for x in range(nx):
                    for k in range(nk):
                        tz, ty, tx, tk = move(z, y, x, k)
                        source = (z * ny + y) * col_devices + x * nk + k
                        target = (tz * ny + ty) * col_devices + tx * nk + tk
                        pairs.append((source, target))
        return lax.ppermute(value, BOTH, pairs)

    def swap_z(value, mask):
        return permute(value, lambda z, y, x, k: (z ^ mask, y, x, k))

    def swap_y(value, mask):
        return permute(value, lambda z, y, x, k: (z, y ^ mask, x, k))

    def swap_x(value, mask):
        return permute(value, lambda z, y, x, k: (z, y, x ^ mask, k))

    def swap_k(value):
        return permute(value, lambda z, y, x, k: (z, y, x, k ^ 1))

    def ring(value):
        return permute(
            value, lambda z, y, x, k: ((z + 1) % nz if k == 0 else (z - 1) % nz, y, x, k)
        )

    def natural(parts, place):
        count = len(parts)
        arrays = list(parts)
        bit = 1
        while bit < count:
            hot = (place & bit) != 0
            arrays = [
                jnp.where(hot, arrays[slot ^ bit], arrays[slot]) for slot in range(count)
            ]
            bit *= 2
        return arrays

    def gather_cols(value, place):
        parts = [None] * col_devices
        for mask in range(nx):
            near = value if mask == 0 else swap_x(value, mask)
            parts[mask * nk] = near
            parts[mask * nk + 1] = swap_k(near)
        return natural(parts, place)

    def scatter_rest(kept, place_x):
        near = lax.dynamic_index_in_dim(kept, place_x, 0, keepdims=False)
        for mask in range(1, nx):
            away = lax.dynamic_index_in_dim(kept, place_x ^ mask, 0, keepdims=False)
            near = near + swap_x(away.astype(BF), mask).astype(F32)
        return near

    def scatter_cols(blocks, place_x, place_k, make):
        hot = place_k == 0
        away = jnp.where(hot, blocks[:, 1], blocks[:, 0])
        near = jnp.where(hot, blocks[:, 0], blocks[:, 1])
        got = swap_k(make(away).astype(BF))
        kept = make(near) + got.astype(F32)
        return scatter_rest(kept, place_x)

    def sum_all(value):
        for mask_count, swap in ((nx, swap_x), (ny, swap_y), (nz, swap_z)):
            bit = 1
            while bit < mask_count:
                value = value + swap(value, bit)
                bit *= 2
        return value + swap_k(value)

    def sum_cols(value):
        value = value + swap_k(value.astype(BF)).astype(F32)
        bit = 1
        while bit < nx:
            value = value + swap_x(value.astype(BF), bit).astype(F32)
            bit *= 2
        return value

    MASKS = [(mx, my) for mx in range(nx) for my in range(ny)]

    def spread_weight(own, x_first):
        parts = {(0, 0): own}
        if x_first:
            for mx in range(1, nx):
                parts[(mx, 0)] = swap_x(own, mx)
            for mx in range(nx):
                for my in range(1, ny):
                    parts[(mx, my)] = swap_y(parts[(mx, 0)], my)
        else:
            for my in range(1, ny):
                parts[(0, my)] = swap_y(own, my)
            for my in range(ny):
                for mx in range(1, nx):
                    parts[(mx, my)] = swap_x(parts[(0, my)], mx)
        return [parts[mask] for mask in MASKS]

    def reduce_weight(parts, x_first):
        sums = dict(zip(MASKS, parts))
        if x_first:
            for my in reversed(range(ny)):
                total = sums[(0, my)].astype(F32)
                for mx in range(1, nx):
                    total = total + swap_x(sums[(mx, my)], mx).astype(F32)
                sums[(0, my)] = total.astype(BF)
            total = sums[(0, 0)].astype(F32)
            for my in range(1, ny):
                total = total + swap_y(sums[(0, my)], my).astype(F32)
        else:
            for mx in reversed(range(nx)):
                total = sums[(mx, 0)].astype(F32)
                for my in range(1, ny):
                    total = total + swap_y(sums[(mx, my)], my).astype(F32)
                sums[(mx, 0)] = total.astype(BF)
            total = sums[(0, 0)].astype(F32)
            for mx in range(1, nx):
                total = total + swap_x(sums[(mx, 0)], mx).astype(F32)
        return total.astype(BF)

    def exchange(value, axis):
        return lax.all_to_all(value, axis, 0, 0, tiled=True)

    def shards(
        tokens,
        gain_attn,
        gain_mlp,
        w_q,
        w_kv,
        a_qkv,
        b_q,
        b_kv,
        w_o,
        a_o,
        b_o,
        w_gate,
        w_up,
        a_gu,
        b_gate,
        b_up,
        w_down,
        a_down,
        b_down,
        lengths,
        teacher,
        out_grad,
    ):
        row_place = lax.axis_index("rows")
        col_place = lax.axis_index("cols")
        place_x = col_place // nk
        place_k = col_place % nk
        row_count, local_features = tokens.shape
        features = local_features * col_devices
        seq_len = row_count * row_devices // lengths.shape[0]
        seqs_here = row_count // seq_len
        own_rows = row_count // col_devices
        rank = a_qkv.shape[1]
        block_d = w_q.shape[0]
        block_r = b_q.shape[0]
        block_e = block_d + block_r
        q_width = w_q.shape[1]
        kv_width = w_kv.shape[1]
        head_size = kv_width * col_devices // 2
        heads_here = q_width // head_size
        hidden_part = w_gate.shape[1] // row_devices
        lens_here = lax.dynamic_slice_in_dim(lengths, row_place * seqs_here, seqs_here)

        gain_rows = jnp.concatenate(
            [gain_attn[None], gain_mlp[None], jnp.zeros((14, local_features), BF)], axis=0
        )
        small_parts = gather_cols(jnp.concatenate([b_o, b_down, gain_rows], axis=0), col_place)
        small_full = jnp.concatenate(small_parts, axis=1)
        gain_one = small_full[2 * block_r].astype(F32)[None]
        gain_two = small_full[2 * block_r + 1].astype(F32)[None]
        full_x = jnp.concatenate(gather_cols(tokens, col_place), axis=1)

        pack_one = jnp.concatenate(
            [
                jnp.concatenate([w_q, w_kv, a_qkv], axis=1),
                jnp.concatenate([b_q, b_kv, jnp.zeros((block_r, rank), BF)], axis=1),
            ],
            axis=0,
        )
        got_one = lax.all_gather(pack_one, "rows", axis=0, tiled=False)
        full_a_qkv = got_one[:, :block_d, q_width + kv_width :].reshape(features, rank)
        qkv_base = got_one[:, :block_d, : q_width + kv_width].reshape(
            features, q_width + kv_width
        )
        full_b_qkv = got_one[:, block_d:, : q_width + kv_width].reshape(rank, q_width + kv_width)
        w_qkv = (qkv_base.astype(F32) + product(full_a_qkv, full_b_qkv)).astype(BF)

        pack_two = jnp.concatenate(
            [
                jnp.concatenate([w_o.T, a_o.T], axis=0),
                jnp.concatenate(
                    [
                        small_full[: 2 * block_r].reshape(-1, q_width),
                        a_gu.reshape(-1, q_width),
                    ],
                    axis=0,
                ),
            ],
            axis=0,
        )
        got_two = lax.all_gather(pack_two, "rows", axis=0, tiled=False)
        o_base = got_two[:, :block_d].reshape(features, q_width)
        full_a_o_t = got_two[:, block_d:block_e].reshape(rank, q_width)
        b_rows = 2 * block_r * features // q_width
        b_pair = got_two[:, block_e : block_e + b_rows].reshape(
            row_devices, 2, block_r, features
        )
        full_b_o = b_pair[:, 0].reshape(rank, features)
        full_b_down = b_pair[:, 1].reshape(rank, features)
        full_a_gu = got_two[:, block_e + b_rows :].reshape(features, rank)
        w_o_t = (o_base.astype(F32) + left_trans(full_b_o, full_a_o_t)).astype(BF)

        def hidden_slices(weight, adapter, x_first):
            block = jnp.concatenate([weight, adapter], axis=0)
            block = block.reshape(block_e, row_devices, hidden_part).transpose(1, 0, 2)
            return spread_weight(exchange(block, "rows"), x_first)

        def joined(parts, factor):
            whole = jnp.concatenate(parts, axis=2)
            width = whole.shape[2]
            base = whole[:, :block_d].reshape(features, width)
            side = whole[:, block_d:].reshape(rank, width)
            return ((base.astype(F32) + product(factor, side)).astype(BF), side)

        full_b_down_t = full_b_down.T
        gate_w, gate_side = joined(hidden_slices(w_gate, b_gate, False), full_a_gu)
        up_w, up_side = joined(hidden_slices(w_up, b_up, True), full_a_gu)
        down_w, down_side = joined(hidden_slices(w_down.T, a_down.T, False), full_b_down_t)

        pair = jnp.stack([teacher, out_grad]).reshape(
            2, col_devices, own_rows, local_features
        )
        pair = exchange(pair.transpose(1, 0, 2, 3), "cols")
        pair = pair.transpose(1, 2, 0, 3).reshape(2, own_rows, features)
        teacher_own = pair[0].astype(F32)
        out_grad_own = pair[1].astype(F32)

        normed, scale_one = norm_forward(full_x.astype(F32), gain_one)
        kv_piece = product(normed, w_qkv[:, q_width:])
        kv_parts = gather_cols(kv_piece, col_place)
        q_lin = product(normed, w_qkv[:, :q_width])
        kv_lin = jnp.concatenate(kv_parts, axis=1)
        query_scale = head_size ** (-0.5)
        cosine_table, sine_table = angles(seq_len, head_size)
        queries = q_lin.reshape(seqs_here, seq_len, heads_here, head_size).transpose(0, 2, 1, 3)
        queries = (rotate(queries, cosine_table, sine_table) * query_scale).astype(BF)
        keys = rotate(
            kv_lin[:, :head_size].reshape(seqs_here, seq_len, head_size),
            cosine_table,
            sine_table,
        ).astype(BF)
        values = kv_lin[:, head_size:].reshape(seqs_here, seq_len, head_size).astype(BF)
        forward_parts = [
            attend_forward(queries[s], keys[s], values[s], lens_here[s])
            for s in range(seqs_here)
        ]
        attn_rows = jnp.concatenate(
            [part[0].transpose(1, 0, 2).reshape(seq_len, q_width) for part in forward_parts],
            axis=0,
        )
        branch_one = scatter_cols(
            attn_rows.reshape(nx, nk, own_rows, q_width),
            place_x,
            place_k,
            lambda block: right_trans(block.reshape(nx * own_rows, q_width), w_o_t).reshape(
                nx, own_rows, features
            ),
        )
        own_x = lax.dynamic_slice_in_dim(full_x, col_place * own_rows, own_rows, 0).astype(F32)
        own_scale = lax.dynamic_slice_in_dim(scale_one, col_place * own_rows, own_rows, 0)
        middle = own_x + branch_one
        middle_low = middle.astype(BF).astype(F32)
        normed_two, scale_two = norm_forward(middle_low, gain_two)

        def gather_ring(value):
            chunks = []
            for step in range(nz):
                chunks.append(jnp.concatenate([value, swap_k(value)], axis=0))
                if step + 1 < nz:
                    value = ring(value)
            return chunks

        def scatter_ring(parts):
            def chip_sum(part):
                return part[:own_rows] + swap_k(part[own_rows:].astype(BF)).astype(F32)

            total = None
            for step in list(range(1, nz)) + [0]:
                mine = chip_sum(parts[step])
                if total is not None:
                    mine = mine + ring(total.astype(BF)).astype(F32)
                total = mine
            return total

        normed_chunks = gather_ring(normed_two)
        gates, ups, hiddens, parts = [], [], [], []
        for chunk in normed_chunks:
            gate_lin = product(chunk, gate_w)
            up_lin = product(chunk, up_w)
            hidden = geglu(gate_lin, up_lin).astype(BF)
            gates.append(gate_lin)
            ups.append(up_lin)
            hiddens.append(hidden)
            parts.append(right_trans(hidden, down_w))
        result = middle + scatter_ring(parts)

        spots = col_place * own_rows + jnp.arange(own_rows)
        limits = jnp.take(lens_here, spots // seq_len) if seqs_here > 1 else lens_here[0]
        valid_rows = ((spots % seq_len) < limits).astype(F32)[:, None]
        valid_count = jnp.sum(lengths).astype(F32)
        error_rows = result - teacher_own
        square = jnp.sum(error_rows * error_rows * valid_rows)
        total_tokens = row_count * row_devices
        seed_grad = out_grad_own + total_tokens / valid_count * error_rows * valid_rows
        grad_two = seed_grad.astype(BF)

        def to_columns(value):
            blocks = value.reshape(own_rows, col_devices, local_features).transpose(1, 0, 2)
            return exchange(blocks, "cols").reshape(row_count, local_features)

        output = to_columns(result.astype(BF))

        grad_chunks = gather_ring(grad_two)
        d_gates, d_ups, back_parts = [], [], []
        for chunk, gate_lin, up_lin in zip(grad_chunks, gates, ups):
            d_hidden = product(chunk, down_w)
            _, geglu_back = jax.vjp(geglu, gate_lin, up_lin)
            d_gate, d_up = geglu_back(d_hidden)
            d_gate = d_gate.astype(BF)
            d_up = d_up.astype(BF)
            d_gates.append(d_gate)
            d_ups.append(d_up)
            back_parts.append(right_trans(d_gate, gate_w) + right_trans(d_up, up_w))
        d_normed_two = scatter_ring(back_parts)

        def weight_grads(left_chunks, right_chunks, factor, x_first):
            left = jnp.concatenate(left_chunks, axis=0)
            right = jnp.concatenate(right_chunks, axis=0)
            whole = left_trans(left, right).astype(BF)
            side = left_trans(factor, whole).astype(BF)
            packed = jnp.concatenate(
                [
                    whole.reshape(row_devices, block_d, -1),
                    side.reshape(row_devices, block_r, -1),
                ],
                axis=1,
            )
            split = [
                packed[:, :, i * hidden_part : (i + 1) * hidden_part] for i in range(len(MASKS))
            ]
            own = exchange(reduce_weight(split, x_first), "rows")
            block = own.transpose(1, 0, 2).reshape(block_e, row_devices * hidden_part)
            return (block[:block_d], block[block_d:], whole)

        down_g, down_s, down_all = weight_grads(grad_chunks, hiddens, full_b_down_t, False)
        gate_g, gate_s, gate_all = weight_grads(normed_chunks, d_gates, full_a_gu, True)
        up_g, up_s, up_all = weight_grads(normed_chunks, d_ups, full_a_gu, False)
        a_gu_part = right_trans(gate_all, gate_side) + right_trans(up_all, up_side)
        b_down_part = right_trans(down_side, down_all)

        d_norm_two, gain_two_part = norm_backward(d_normed_two, middle_low, gain_two, scale_two)
        d_middle = seed_grad + d_norm_two

        grad_one = d_middle.astype(BF)
        grad_one_full = jnp.concatenate(gather_cols(grad_one, col_place), axis=0)
        d_attended = product(grad_one_full, w_o_t).astype(BF)
        o_grad_t = left_trans(grad_one_full, attn_rows).astype(BF)
        a_o_grad_t = product(full_b_o, o_grad_t).astype(BF)
        b_o_part = right_trans(full_a_o_t, o_grad_t)

        def split_features(value):
            blocks = value.reshape(rank, nx, nk, local_features).transpose(1, 2, 0, 3)
            own = scatter_cols(blocks, place_x, place_k, lambda block: block)
            return own.astype(BF).reshape(row_devices, block_r, local_features)

        rows_pack = jnp.concatenate(
            [
                o_grad_t.reshape(row_devices, block_d, q_width),
                a_o_grad_t.reshape(row_devices, block_r, q_width),
                split_features(b_o_part),
                split_features(b_down_part),
                a_gu_part.astype(BF).reshape(row_devices, -1, q_width),
            ],
            axis=1,
        )
        rows_sum = lax.psum_scatter(rows_pack, "rows", scatter_dimension=0, tiled=True)[0]
        grad_w_o = rows_sum[:block_d].T.astype(F32)
        grad_a_o = rows_sum[block_d:block_e].T.astype(F32)
        grad_b_o = rows_sum[block_e : block_e + block_r].astype(F32)
        grad_b_down = rows_sum[block_e + block_r : block_e + 2 * block_r].astype(F32)
        grad_a_gu = sum_cols(
            rows_sum[block_e + 2 * block_r :].reshape(block_d, rank).astype(F32)
        )

        d_heads = d_attended.reshape(seqs_here, seq_len, heads_here, head_size)
        d_heads = d_heads.transpose(0, 2, 1, 3)
        q_pieces, kv_pieces = [], []
        for s in range(seqs_here):
            d_query, d_key, d_value = attend_backward(
                queries[s], keys[s], values[s], lens_here[s], forward_parts[s][1], d_heads[s]
            )
            d_query = rotate(d_query * query_scale, cosine_table, -sine_table)
            q_pieces.append(d_query.transpose(1, 0, 2).reshape(seq_len, q_width).astype(BF))
            d_key = rotate(d_key, cosine_table, -sine_table)
            kv_pieces.append(jnp.concatenate([d_key, d_value], axis=1))
        d_q_lin = jnp.concatenate(q_pieces, axis=0)
        kv_blocks = jnp.concatenate(kv_pieces, axis=0).reshape(row_count, nx, nk, kv_width)
        d_kv_lin = scatter_cols(
            kv_blocks.transpose(1, 2, 0, 3), place_x, place_k, lambda block: block
        ).astype(BF)
        d_qkv = jnp.concatenate([d_q_lin, d_kv_lin], axis=1)
        d_normed = scatter_cols(
            d_qkv.reshape(nx, nk, own_rows, q_width + kv_width),
            place_x,
            place_k,
            lambda block: right_trans(
                block.reshape(nx * own_rows, q_width + kv_width), w_qkv
            ).reshape(nx, own_rows, features),
        )
        qkv_grad = left_trans(normed, d_qkv).astype(BF)
        b_qkv_grad = left_trans(full_a_qkv, qkv_grad).astype(BF)
        a_qkv_part = right_trans(qkv_grad, full_b_qkv).astype(BF)
        last_pack = jnp.concatenate(
            [
                jnp.concatenate(
                    [
                        qkv_grad.reshape(row_devices, block_d, -1),
                        a_qkv_part.reshape(row_devices, block_d, rank),
                    ],
                    axis=2,
                ),
                jnp.concatenate(
                    [
                        b_qkv_grad.reshape(row_devices, block_r, -1),
                        jnp.zeros((row_devices, block_r, rank), BF),
                    ],
                    axis=2,
                ),
            ],
            axis=1,
        )
        last_sum = lax.psum_scatter(last_pack, "rows", scatter_dimension=0, tiled=True)[0]
        grad_a_qkv = sum_cols(last_sum[:block_d, q_width + kv_width :].astype(F32))
        grad_w_q = last_sum[:block_d, :q_width].astype(F32)
        grad_w_kv = last_sum[:block_d, q_width : q_width + kv_width].astype(F32)
        grad_b_q = last_sum[block_d:, :q_width].astype(F32)
        grad_b_kv = last_sum[block_d:, q_width : q_width + kv_width].astype(F32)

        d_norm_one, gain_one_part = norm_backward(d_normed, own_x, gain_one, own_scale)
        grad_tokens = to_columns((d_middle + d_norm_one).astype(BF)).astype(F32)
        vectors = jnp.concatenate(
            [
                gain_one_part[None],
                gain_two_part[None],
                jnp.full((1, features), square, F32),
            ],
            axis=0,
        )
        sums = sum_all(vectors)
        gains = lax.dynamic_slice_in_dim(sums, col_place * local_features, local_features, 1)
        loss_value = (sums[2, 0] / (2.0 * valid_count)).reshape(1)
        return (
            output,
            loss_value,
            grad_tokens,
            gains[0],
            gains[1],
            grad_w_q,
            grad_w_kv,
            grad_a_qkv,
            grad_b_q,
            grad_b_kv,
            grad_w_o,
            grad_a_o,
            grad_b_o,
            gate_g.astype(F32),
            up_g.astype(F32),
            grad_a_gu,
            gate_s.astype(F32),
            up_s.astype(F32),
            down_g.T.astype(F32),
            down_s.T.astype(F32),
            grad_b_down,
        )

    in_specs = (
        P("rows", "cols"),
        P("cols"),
        P("cols"),
        P("rows", "cols"),
        P("rows", "cols"),
        P("rows", None),
        P("rows", "cols"),
        P("rows", "cols"),
        P("cols", "rows"),
        P("cols", "rows"),
        P("rows", "cols"),
        P("rows", "cols"),
        P("rows", "cols"),
        P("rows", None),
        P("rows", "cols"),
        P("rows", "cols"),
        P("cols", "rows"),
        P("cols", "rows"),
        P("rows", "cols"),
        P(),
        P("rows", "cols"),
        P("rows", "cols"),
    )
    out_specs = (
        P("rows", "cols"),
        P(),
        P("rows", "cols"),
        P("cols"),
        P("cols"),
        P("rows", "cols"),
        P("rows", "cols"),
        P("rows", None),
        P("rows", "cols"),
        P("rows", "cols"),
        P("cols", "rows"),
        P("cols", "rows"),
        P("rows", "cols"),
        P("rows", "cols"),
        P("rows", "cols"),
        P("rows", None),
        P("rows", "cols"),
        P("rows", "cols"),
        P("cols", "rows"),
        P("cols", "rows"),
        P("rows", "cols"),
    )
    return jax.shard_map(shards, mesh=mesh, in_specs=in_specs, out_specs=out_specs, check_vma=False)
```

```python
import jax
import jax.numpy as jnp
from jax import lax
from jax.sharding import PartitionSpec as P

NORM_EPS = 1e-06
BF = jnp.bfloat16
F32 = jnp.float32


def product(former, latter):
    return jnp.dot(former, latter, preferred_element_type=F32)


def left_trans(former, latter):
    return lax.dot_general(
        former, latter, (((0,), (0,)), ((), ())), preferred_element_type=F32
    )


def right_trans(former, latter):
    return lax.dot_general(
        former, latter, (((1,), (1,)), ((), ())), preferred_element_type=F32
    )


def angles(length, head_size):
    half_size = head_size // 2
    inverse = 10000.0 ** (-(jnp.arange(half_size, dtype=F32) * 2.0 / head_size))
    theta = jnp.arange(length, dtype=F32)[:, None] * inverse[None, :]
    return (jnp.cos(theta), jnp.sin(theta))


def rotate(values_in, cosine_table, sine_table):
    half_size = values_in.shape[-1] // 2
    first_half = values_in[..., :half_size]
    second_half = values_in[..., half_size:]
    return jnp.concatenate(
        [
            first_half * cosine_table - second_half * sine_table,
            second_half * cosine_table + first_half * sine_table,
        ],
        axis=-1,
    )


def allowed_mask(key_count, length):
    row_place = jnp.arange(key_count)[:, None]
    col_place = jnp.arange(key_count)[None, :]
    return ((col_place <= row_place) & (col_place < length))[None]


def attend_forward(query_rows, key_rows, value_rows, length):
    allowed = allowed_mask(key_rows.shape[0], length)
    scores = jnp.einsum("hqd,kd->hqk", query_rows, key_rows, preferred_element_type=F32)
    masked = jnp.where(allowed, scores, -1e30)
    largest = jnp.max(masked, axis=-1, keepdims=True)
    exponent = jnp.exp(masked - largest)
    totals = jnp.sum(exponent, axis=-1, keepdims=True)
    probability = (exponent / totals).astype(BF)
    attended = jnp.einsum("hqk,kd->hqd", probability, value_rows, preferred_element_type=F32)
    return (attended.astype(BF), (largest + jnp.log(totals))[..., 0])


def attend_backward(query_rows, key_rows, value_rows, length, log_total, grad_out):
    allowed = allowed_mask(key_rows.shape[0], length)
    scores = jnp.einsum("hqd,kd->hqk", query_rows, key_rows, preferred_element_type=F32)
    probability = jnp.where(allowed, jnp.exp(scores - log_total[..., None]), 0.0)
    grad_prob = jnp.einsum("hqd,kd->hqk", grad_out, value_rows, preferred_element_type=F32)
    row_terms = jnp.sum(probability * grad_prob, axis=-1, keepdims=True)
    grad_scores = (probability * (grad_prob - row_terms)).astype(BF)
    grad_query = jnp.einsum("hqk,kd->hqd", grad_scores, key_rows, preferred_element_type=F32)
    grad_key = jnp.einsum("hqk,hqd->kd", grad_scores, query_rows, preferred_element_type=F32)
    grad_value = jnp.einsum(
        "hqk,hqd->kd", probability.astype(BF), grad_out, preferred_element_type=F32
    )
    return (grad_query, grad_key, grad_value)


def norm_scale(values_in):
    return lax.rsqrt(jnp.mean(values_in * values_in, axis=-1, keepdims=True) + NORM_EPS)


def norm_forward(values_in, gain_row):
    row_scale = norm_scale(values_in)
    return ((values_in * row_scale * (1.0 + gain_row)).astype(BF), row_scale)


def norm_backward(grad_rows, rows_in, gain_row, row_scale):
    factor = 1.0 + gain_row
    row_dots = jnp.sum(grad_rows * factor * rows_in, axis=-1, keepdims=True)
    grad_input = (
        row_scale * factor * grad_rows
        - rows_in * (row_scale * row_scale * row_scale) * row_dots / rows_in.shape[1]
    )
    return (grad_input, jnp.sum(grad_rows * rows_in * row_scale, axis=0))


def geglu(gate_lin, up_lin):
    return jax.nn.gelu(gate_lin, approximate=True) * up_lin


def solution(mesh):
    row_devices = mesh.shape["rows"]
    col_devices = mesh.shape["cols"]
    nk = 2
    nx = col_devices // nk
    nz = 4 if row_devices % 4 == 0 else row_devices
    ny = row_devices // nz
    BOTH = ("rows", "cols")

    def permute(value, move):
        pairs = []
        for z in range(nz):
            for y in range(ny):
                for x in range(nx):
                    for k in range(nk):
                        tz, ty, tx, tk = move(z, y, x, k)
                        source = (z * ny + y) * col_devices + x * nk + k
                        target = (tz * ny + ty) * col_devices + tx * nk + tk
                        pairs.append((source, target))
        return lax.ppermute(value, BOTH, pairs)

    def swap_z(value, mask):
        return permute(value, lambda z, y, x, k: (z ^ mask, y, x, k))

    def swap_y(value, mask):
        return permute(value, lambda z, y, x, k: (z, y ^ mask, x, k))

    def swap_x(value, mask):
        return permute(value, lambda z, y, x, k: (z, y, x ^ mask, k))

    def swap_k(value):
        return permute(value, lambda z, y, x, k: (z, y, x, k ^ 1))

    def ring(value):
        return permute(
            value, lambda z, y, x, k: ((z + 1) % nz if k == 0 else (z - 1) % nz, y, x, k)
        )

    def natural(parts, place):
        count = len(parts)
        arrays = list(parts)
        bit = 1
        while bit < count:
            hot = (place & bit) != 0
            arrays = [
                jnp.where(hot, arrays[slot ^ bit], arrays[slot]) for slot in range(count)
            ]
            bit *= 2
        return arrays

    def gather_cols(value, place):
        parts = [None] * col_devices
        for mask in range(nx):
            near = value if mask == 0 else swap_x(value, mask)
            parts[mask * nk] = near
            parts[mask * nk + 1] = swap_k(near)
        return natural(parts, place)

    def scatter_rest(kept, place_x):
        near = lax.dynamic_index_in_dim(kept, place_x, 0, keepdims=False)
        for mask in range(1, nx):
            away = lax.dynamic_index_in_dim(kept, place_x ^ mask, 0, keepdims=False)
            near = near + swap_x(away.astype(BF), mask).astype(F32)
        return near

    def scatter_cols(blocks, place_x, place_k, make):
        hot = place_k == 0
        away = jnp.where(hot, blocks[:, 1], blocks[:, 0])
        near = jnp.where(hot, blocks[:, 0], blocks[:, 1])
        got = swap_k(make(away).astype(BF))
        kept = make(near) + got.astype(F32)
        return scatter_rest(kept, place_x)

    def row_parts(value):
        parts = []
        for mask_z in range(nz):
            near = value if mask_z == 0 else swap_z(value, mask_z)
            parts.append(near)
            parts.extend(swap_y(near, mask) for mask in range(1, ny))
        return parts

    def scatter_y(blocks, place_y):
        blocks = blocks.reshape(nz, ny, *blocks.shape[1:])
        kept = lax.dynamic_index_in_dim(blocks, place_y, 1, keepdims=False)
        got = []
        for mask in range(1, ny):
            away = lax.dynamic_index_in_dim(blocks, place_y ^ mask, 1, keepdims=False)
            got.append(swap_y(away, mask))
        return [kept] + got

    def scatter_z(parts, place_z):
        kept = sum(part.astype(F32) for part in parts)
        got = [lax.dynamic_index_in_dim(kept, place_z, 0, keepdims=False)]
        for mask in range(1, nz):
            away = lax.dynamic_index_in_dim(kept, place_z ^ mask, 0, keepdims=False)
            got.append(swap_z(away.astype(BF), mask))
        return got

    def total(parts):
        return sum(part.astype(F32) for part in parts)

    def sum_all(value):
        for mask_count, swap in ((nz, swap_z), (ny, swap_y), (nx, swap_x)):
            bit = 1
            while bit < mask_count:
                value = value + swap(value, bit)
                bit *= 2
        return value + swap_k(value)

    def after(value, *others):
        return lax.optimization_barrier((value, *others))[0]

    def spread_x(own):
        return [own] + [swap_x(own, mask) for mask in range(1, nx)]

    def exchange(value, axis):
        return lax.all_to_all(value, axis, 0, 0, tiled=True)

    def shards(
        tokens,
        gain_attn,
        gain_mlp,
        w_q,
        w_kv,
        a_qkv,
        b_q,
        b_kv,
        w_o,
        a_o,
        b_o,
        w_gate,
        w_up,
        a_gu,
        b_gate,
        b_up,
        w_down,
        a_down,
        b_down,
        lengths,
        teacher,
        out_grad,
    ):
        row_place = lax.axis_index("rows")
        col_place = lax.axis_index("cols")
        place_x = col_place // nk
        place_z = row_place // ny
        place_y = row_place % ny
        place_k = col_place % nk
        row_count, local_features = tokens.shape
        features = local_features * col_devices
        seq_len = row_count * row_devices // lengths.shape[0]
        seqs_here = row_count // seq_len
        own_rows = row_count // col_devices
        rank = a_qkv.shape[1]
        block_d = w_q.shape[0]
        block_r = b_q.shape[0]
        block_e = block_d + block_r
        q_width = w_q.shape[1]
        kv_width = w_kv.shape[1]
        head_size = kv_width * col_devices // 2
        heads_here = q_width // head_size
        hidden_part = w_gate.shape[1] // row_devices
        lens_here = lax.dynamic_slice_in_dim(lengths, row_place * seqs_here, seqs_here)

        gain_rows = jnp.concatenate(
            [gain_attn[None], gain_mlp[None], jnp.zeros((14, local_features), BF)], axis=0
        )
        gain_full = jnp.concatenate(gather_cols(gain_rows, col_place), axis=1).astype(F32)
        gain_one = gain_full[0:1]
        gain_two = gain_full[1:2]
        full_x = jnp.concatenate(gather_cols(tokens, col_place), axis=1)

        pack_one = jnp.concatenate(
            [
                jnp.concatenate([w_q, w_kv, a_qkv], axis=1),
                jnp.concatenate([b_q, b_kv, jnp.zeros((block_r, rank), BF)], axis=1),
            ],
            axis=0,
        )
        got_one = jnp.stack(natural(row_parts(pack_one), row_place))
        slice_r = rank // col_devices
        own_a_gu = lax.dynamic_slice_in_dim(a_gu, col_place * slice_r, slice_r, 1)
        wide = lax.all_gather(
            jnp.concatenate([b_o, b_down, own_a_gu.reshape(-1, local_features)], axis=0),
            BOTH,
            axis=0,
            tiled=False,
        )

        def hidden_blocks(value):
            blocks = value.reshape(value.shape[0], row_devices, hidden_part)
            return blocks.transpose(1, 0, 2)

        def hidden_slice(value):
            return exchange(value, "rows").reshape(features, hidden_part)

        side_blocks = jnp.stack(
            [hidden_blocks(b_gate), hidden_blocks(b_up), hidden_blocks(a_down.T)], axis=1
        )
        normed, scale_one = norm_forward(full_x.astype(F32), gain_one)
        gate_own = hidden_slice(hidden_blocks(w_gate))
        pack_two = jnp.concatenate([w_o.T, a_o.T], axis=0)
        pack_two, side_blocks, gate_own, got_one = lax.optimization_barrier(
            (pack_two, side_blocks, gate_own, got_one)
        )
        parts_two = row_parts(pack_two)
        gate_parts = spread_x(gate_own)
        side_own = exchange(side_blocks, "rows")
        full_a_qkv = got_one[:, :block_d, q_width + kv_width :].reshape(features, rank)
        qkv_base = got_one[:, :block_d, : q_width + kv_width].reshape(
            features, q_width + kv_width
        )
        full_b_qkv = got_one[:, block_d:, : q_width + kv_width].reshape(rank, q_width + kv_width)
        w_qkv = (qkv_base.astype(F32) + product(full_a_qkv, full_b_qkv)).astype(BF)

        kv_piece = product(normed, w_qkv[:, q_width:])
        kv_parts = gather_cols(kv_piece, col_place)
        q_lin = product(normed, w_qkv[:, :q_width])
        kv_lin = jnp.concatenate(kv_parts, axis=1)
        up_blocks, side_own, q_lin = lax.optimization_barrier(
            (hidden_blocks(w_up), side_own, q_lin)
        )
        up_own = hidden_slice(up_blocks)
        side_parts = spread_x(side_own.transpose(1, 0, 2, 3).reshape(3, rank, hidden_part))
        query_scale = head_size ** (-0.5)
        cosine_table, sine_table = angles(seq_len, head_size)
        queries = q_lin.reshape(seqs_here, seq_len, heads_here, head_size).transpose(0, 2, 1, 3)
        queries = (rotate(queries, cosine_table, sine_table) * query_scale).astype(BF)
        keys = rotate(
            kv_lin[:, :head_size].reshape(seqs_here, seq_len, head_size),
            cosine_table,
            sine_table,
        ).astype(BF)
        values = kv_lin[:, head_size:].reshape(seqs_here, seq_len, head_size).astype(BF)
        forward_parts = [
            attend_forward(queries[s], keys[s], values[s], lens_here[s])
            for s in range(seqs_here)
        ]
        attn_rows = jnp.concatenate(
            [part[0].transpose(1, 0, 2).reshape(seq_len, q_width) for part in forward_parts],
            axis=0,
        )
        attn_rows, up_own, gate_parts, wide, *parts_two = lax.optimization_barrier(
            (attn_rows, up_own, gate_parts, wide, *parts_two)
        )
        up_parts = spread_x(up_own)
        down_blocks, up_own = lax.optimization_barrier((hidden_blocks(w_down.T), up_own))
        down_own = hidden_slice(down_blocks)
        got_two = jnp.stack(natural(parts_two, row_place))
        o_base = got_two[:, :block_d].reshape(features, q_width)
        full_a_o_t = got_two[:, block_d:block_e].reshape(rank, q_width)
        wide = wide.reshape(row_devices, col_devices, -1, local_features)

        def whole_b(start):
            value = wide[:, :, start : start + block_r]
            return value.transpose(0, 2, 1, 3).reshape(rank, features)

        full_b_o = whole_b(0)
        w_o_t = (o_base.astype(F32) + left_trans(full_b_o, full_a_o_t)).astype(BF)

        def scatter_tokens(rows, weight):
            blocks = rows.reshape(nx, nk, own_rows, rows.shape[1])
            hot = place_k == 0

            def partial_sum(first, second):
                block = jnp.where(hot, blocks[:, first], blocks[:, second])
                return right_trans(block.reshape(nx * own_rows, rows.shape[1]), weight)

            kept = swap_k(partial_sum(1, 0).astype(BF)).astype(F32) + partial_sum(0, 1)
            kept = kept.reshape(nx, own_rows, features)
            sent = [
                lax.dynamic_index_in_dim(kept, place_x ^ mask, 0, keepdims=False).astype(BF)
                for mask in range(1, nx)
            ]
            return (lax.dynamic_index_in_dim(kept, place_x, 0, keepdims=False), sent)

        def finish_tokens(near, sent):
            return near + total([swap_x(value, i + 1) for i, value in enumerate(sent)])

        near_one, sent_one = scatter_tokens(attn_rows, w_o_t)
        up_parts, side_parts, sent_one = lax.optimization_barrier(
            (up_parts, side_parts, sent_one)
        )
        branch_one = finish_tokens(near_one, sent_one)
        own_x = lax.dynamic_slice_in_dim(full_x, col_place * own_rows, own_rows, 0).astype(F32)
        own_scale = lax.dynamic_slice_in_dim(scale_one, col_place * own_rows, own_rows, 0)
        middle = own_x + branch_one
        down_own, middle = lax.optimization_barrier((down_own, middle))
        full_b_down = whole_b(block_r)
        full_b_down_t = full_b_down.T
        full_a_gu = wide[:, :, 2 * block_r :].reshape(row_devices, col_devices, block_d, slice_r)
        full_a_gu = full_a_gu.transpose(0, 2, 1, 3).reshape(features, rank)
        gate_sides = [part[0] for part in side_parts]
        up_sides = [part[1] for part in side_parts]
        down_sides = [part[2] for part in side_parts]

        def joined(bases, sides, factor):
            parts = [
                (base.astype(F32) + product(factor, side)).astype(BF)
                for base, side in zip(bases, sides)
            ]
            return jnp.concatenate(parts, axis=1)

        middle_low = middle.astype(BF).astype(F32)
        normed_two, scale_two = norm_forward(middle_low, gain_two)

        def gather_ring(value):
            chunks = []
            for step in range(nz):
                lines = [swap_y(value, mask) for mask in range(1, ny)]
                near = value
                if step + 1 < nz:
                    value = ring(value)
                    lines, value = lax.optimization_barrier((lines, value))
                for line in [near] + lines:
                    chunks.append(jnp.concatenate([line, swap_k(line)], axis=0))
            return chunks

        def scatter_ring(parts):
            totals = []
            for step in list(range(1, nz)) + [0]:
                mine = None
                for mask in reversed(range(ny)):
                    part = parts[step * ny + mask]
                    away = swap_k(part[own_rows:].astype(BF))
                    chip = part[:own_rows] + away.astype(F32)
                    if mask:
                        chip = swap_y(chip.astype(BF), mask).astype(F32)
                    mine = chip if mine is None else mine + chip
                if totals:
                    mine = mine + ring(totals[-1]).astype(F32)
                totals.append(mine.astype(BF) if step else mine)
            return totals

        normed_chunks = gather_ring(normed_two)
        gate_w = joined(gate_parts, gate_sides, full_a_gu)
        up_w = joined(up_parts, up_sides, full_a_gu)
        down_parts = spread_x(down_own)
        down_parts, normed_chunks[-ny] = lax.optimization_barrier(
            (down_parts, normed_chunks[-ny])
        )
        down_w = joined(down_parts, down_sides, full_b_down_t)
        pair = jnp.stack([teacher, out_grad]).reshape(
            2, col_devices, own_rows, local_features
        )
        pair = exchange(after(pair.transpose(1, 0, 2, 3), down_own), "cols")
        gates, ups, hiddens, parts = [], [], [], []
        for chunk in normed_chunks:
            gate_lin = product(chunk, gate_w)
            up_lin = product(chunk, up_w)
            hidden = geglu(gate_lin, up_lin).astype(BF)
            gates.append(gate_lin)
            ups.append(up_lin)
            hiddens.append(hidden)
            parts.append(right_trans(hidden, down_w))
        pair, parts[0] = lax.optimization_barrier((pair, parts[0]))
        pair = pair.transpose(1, 2, 0, 3).reshape(2, own_rows, features)
        teacher_own = pair[0].astype(F32)
        out_grad_own = pair[1].astype(F32)
        result = middle + scatter_ring(parts)[-1]

        spots = col_place * own_rows + jnp.arange(own_rows)
        limits = jnp.take(lens_here, spots // seq_len) if seqs_here > 1 else lens_here[0]
        valid_rows = ((spots % seq_len) < limits).astype(F32)[:, None]
        valid_count = jnp.sum(lengths).astype(F32)
        error_rows = result - teacher_own
        square = jnp.sum(error_rows * error_rows * valid_rows)
        total_tokens = row_count * row_devices
        seed_grad = out_grad_own + total_tokens / valid_count * error_rows * valid_rows
        grad_two = seed_grad.astype(BF)

        def to_columns(value):
            blocks = value.reshape(own_rows, col_devices, local_features).transpose(1, 0, 2)
            parts = []
            for mask in range(col_devices):
                block = lax.dynamic_index_in_dim(blocks, col_place ^ mask, 0, keepdims=False)
                if mask:
                    block = permute(
                        block,
                        lambda z, y, x, k, mask=mask: (z, y, x ^ (mask // nk), k ^ (mask % nk)),
                    )
                parts.append(block)
            return jnp.concatenate(natural(parts, col_place), axis=0)


        grad_chunks = gather_ring(grad_two)
        d_gates, d_ups, parts = [], [], []
        for chunk, gate_lin, up_lin in zip(grad_chunks, gates, ups):
            d_hidden = product(chunk, down_w)
            _, geglu_back = jax.vjp(geglu, gate_lin, up_lin)
            d_gate, d_up = geglu_back(d_hidden)
            d_gate = d_gate.astype(BF)
            d_up = d_up.astype(BF)
            d_gates.append(d_gate)
            d_ups.append(d_up)
            if len(d_gates) == 3:
                output = to_columns(after(result.astype(BF), d_gate))
            parts.append(right_trans(d_gate, gate_w) + right_trans(d_up, up_w))
        totals = scatter_ring(parts)
        d_normed_two = totals[-1]

        def weight_grad(left, right, factor, i):
            piece = right[:, i * hidden_part : (i + 1) * hidden_part]
            whole = left_trans(left, piece).astype(BF)
            side = left_trans(factor, whole).astype(BF)
            pack = jnp.concatenate(
                [
                    whole.reshape(row_devices, block_d, hidden_part),
                    side.reshape(row_devices, block_r, hidden_part),
                ],
                axis=1,
            )
            return (pack, whole)

        def weight_grads(left, right, factor):
            pairs = [weight_grad(left, right, factor, i) for i in range(nx)]
            return ([pair[0] for pair in pairs], [pair[1] for pair in pairs])

        def share_x(packs):
            return [swap_x(packs[mask], mask) for mask in range(1, nx)]

        def owned(kept, got):
            return exchange(total([kept] + got).astype(BF), "rows")

        def in_place(own):
            block = jnp.concatenate([own[r] for r in range(row_devices)], axis=1)
            return (block[:block_d].astype(F32), block[block_d:].astype(F32))

        def inner(sides, wholes):
            return sum(right_trans(side, whole) for side, whole in zip(sides, wholes))

        normed_all = jnp.concatenate(normed_chunks, axis=0)
        grad_all = after(jnp.concatenate(grad_chunks, axis=0), parts[-1])
        down_packs, down_all = weight_grads(
            grad_all, jnp.concatenate(hiddens, axis=0), full_b_down_t
        )
        down_got = share_x(down_packs)
        d_norm_two, gain_two_part = norm_backward(d_normed_two, middle_low, gain_two, scale_two)
        d_middle = seed_grad + d_norm_two

        grad_one = d_middle.astype(BF)
        near_parts = spread_x(grad_one)
        gates_all = jnp.concatenate(d_gates, axis=0)
        normed_all, near_parts[0] = lax.optimization_barrier((normed_all, near_parts[0]))
        gate_away = [
            weight_grad(normed_all, gates_all, full_a_gu, i) for i in range(1, nx)
        ]
        gate_away, near_parts, down_got, normed_all = lax.optimization_barrier(
            (gate_away, near_parts, down_got, normed_all)
        )
        gate_near = weight_grad(normed_all, gates_all, full_a_gu, 0)
        gate_packs = [pair[0] for pair in [gate_near] + gate_away]
        gate_all = [pair[1] for pair in [gate_near] + gate_away]
        gate_packs[0], normed_all = lax.optimization_barrier((gate_packs[0], normed_all))
        up_packs, up_all = weight_grads(normed_all, jnp.concatenate(d_ups, axis=0), full_a_gu)
        gate_got = share_x(gate_packs)
        down_g = owned(down_packs[0], down_got)
        grad_parts = []
        for near in near_parts:
            grad_parts.extend([near, swap_k(near)])
        grad_one_full = jnp.concatenate(natural(grad_parts, col_place), axis=0)
        d_attended = product(grad_one_full, w_o_t).astype(BF)
        gate_got, down_g, d_attended = lax.optimization_barrier((gate_got, down_g, d_attended))
        gate_g = owned(gate_packs[0], gate_got)
        up_got = share_x([None] + [after(pack, gate_got[0]) for pack in up_packs[1:]])
        d_heads = d_attended.reshape(seqs_here, seq_len, heads_here, head_size)
        d_heads = d_heads.transpose(0, 2, 1, 3)
        q_pieces, kv_pieces = [], []
        for s in range(seqs_here):
            d_query, d_key, d_value = attend_backward(
                queries[s], keys[s], values[s], lens_here[s], forward_parts[s][1], d_heads[s]
            )
            d_query = rotate(d_query * query_scale, cosine_table, -sine_table)
            q_pieces.append(d_query.transpose(1, 0, 2).reshape(seq_len, q_width).astype(BF))
            d_key = rotate(d_key, cosine_table, -sine_table)
            kv_pieces.append(jnp.concatenate([d_key, d_value], axis=1))
        d_q_lin = jnp.concatenate(q_pieces, axis=0)
        kv_blocks = jnp.concatenate(kv_pieces, axis=0).reshape(row_count, nx, nk, kv_width)
        d_kv_lin = scatter_cols(
            kv_blocks.transpose(1, 2, 0, 3), place_x, place_k, lambda block: block
        ).astype(BF)
        up_got, gate_g, d_kv_lin = lax.optimization_barrier((up_got, gate_g, d_kv_lin))
        up_g = owned(up_packs[0], up_got)
        d_qkv = jnp.concatenate([d_q_lin, d_kv_lin], axis=1)
        near_two, sent = scatter_tokens(d_qkv, w_qkv)
        d_normed = finish_tokens(near_two, sent)

        def blocks_of(value):
            return value.reshape(value.shape[0], nx, nk, -1).transpose(1, 2, 0, 3)

        def rank_blocks(value):
            blocks = value.reshape(nx, nk, slice_r, row_devices, block_d)
            blocks = blocks.transpose(0, 1, 3, 2, 4)
            return blocks.reshape(nx, nk, rank, local_features)

        o_rows = after(grad_one_full, d_q_lin)
        o_grad_t = left_trans(o_rows, attn_rows).astype(BF)
        a_o_grad_t = product(full_b_o, o_grad_t).astype(BF)
        shared = jnp.concatenate(
            [
                blocks_of(right_trans(full_a_o_t, o_grad_t)),
                blocks_of(inner(down_sides, down_all)),
                rank_blocks(
                    inner(gate_sides, gate_all) + inner(up_sides, up_all)
                ),
            ],
            axis=2,
        )
        shared = scatter_cols(shared, place_x, place_k, lambda block: block).astype(BF)
        shared = shared.reshape(3, row_devices, block_r, local_features).transpose(1, 0, 2, 3)
        o_parts = scatter_y(
            jnp.concatenate(
                [
                    o_grad_t.reshape(row_devices, block_d, q_width),
                    a_o_grad_t.reshape(row_devices, block_r, q_width),
                    shared.reshape(row_devices, 3 * block_r, local_features),
                ],
                axis=1,
            ),
            place_y,
        )
        qkv_grad = left_trans(after(normed, sent[0]), d_qkv).astype(BF)
        b_qkv_grad = left_trans(full_a_qkv, qkv_grad).astype(BF)
        a_qkv_part = rank_blocks(right_trans(full_b_qkv, qkv_grad))
        a_qkv_part = scatter_cols(a_qkv_part, place_x, place_k, lambda block: block).astype(BF)
        last_parts = scatter_y(
            jnp.concatenate(
                [
                    qkv_grad.reshape(row_devices, -1, kv_width),
                    b_qkv_grad.reshape(row_devices, -1, kv_width),
                    a_qkv_part.reshape(row_devices, -1, kv_width),
                ],
                axis=1,
            ),
            place_y,
        )
        d_norm_one, gain_one_part = norm_backward(d_normed, own_x, gain_one, own_scale)
        grad_low_x = (d_middle + d_norm_one).astype(BF)
        o_parts, up_g, grad_low_x = lax.optimization_barrier((o_parts, up_g, grad_low_x))
        o_parts = scatter_z(o_parts, place_z)
        grad_tokens = to_columns(grad_low_x).astype(F32)
        vectors = jnp.concatenate(
            [
                gain_one_part[None],
                gain_two_part[None],
                jnp.full((1, features), square, F32),
            ],
            axis=0,
        )
        last_parts, grad_low_x = lax.optimization_barrier((last_parts, grad_low_x))
        last_parts = scatter_z(last_parts, place_z)
        down_g, d_down_side = in_place(down_g)
        gate_g, d_gate_side = in_place(gate_g)
        up_g, d_up_side = in_place(up_g)

        def join_ranks(value):
            value = value.reshape(slice_r, block_d).astype(BF)
            return jnp.concatenate(gather_cols(value, col_place), axis=0).T.astype(F32)

        rows_sum = total(o_parts)
        grad_w_o = rows_sum[:block_d].T
        grad_a_o = rows_sum[block_d:block_e].T
        grad_b_o = rows_sum[block_e : block_e + block_r]
        grad_b_down = rows_sum[block_e + block_r : block_e + 2 * block_r]
        a_gu_own = rows_sum[block_e + 2 * block_r :]
        last_sum = total(last_parts)
        wide_q = q_width + kv_width
        first_cut = block_d * wide_q // kv_width
        second_cut = block_e * wide_q // kv_width
        grad_w_qkv = last_sum[:first_cut].reshape(block_d, wide_q)
        grad_b_qkv = last_sum[first_cut:second_cut].reshape(block_r, wide_q)
        a_qkv_own = last_sum[second_cut:]
        grad_a_gu = join_ranks(a_gu_own)
        grad_a_qkv = join_ranks(a_qkv_own)
        grad_w_q = grad_w_qkv[:, :q_width]
        grad_w_kv = grad_w_qkv[:, q_width:]
        grad_b_q = grad_b_qkv[:, :q_width]
        grad_b_kv = grad_b_qkv[:, q_width:]
        sums = sum_all(vectors)
        gains = lax.dynamic_slice_in_dim(sums, col_place * local_features, local_features, 1)
        loss_value = (sums[2, 0] / (2.0 * valid_count)).reshape(1)
        return (
            output,
            loss_value,
            grad_tokens,
            gains[0],
            gains[1],
            grad_w_q,
            grad_w_kv,
            grad_a_qkv,
            grad_b_q,
            grad_b_kv,
            grad_w_o,
            grad_a_o,
            grad_b_o,
            gate_g,
            up_g,
            grad_a_gu,
            d_gate_side,
            d_up_side,
            down_g.T,
            d_down_side.T,
            grad_b_down,
        )

    in_specs = (
        P("rows", "cols"),
        P("cols"),
        P("cols"),
        P("rows", "cols"),
        P("rows", "cols"),
        P("rows", None),
        P("rows", "cols"),
        P("rows", "cols"),
        P("cols", "rows"),
        P("cols", "rows"),
        P("rows", "cols"),
        P("rows", "cols"),
        P("rows", "cols"),
        P("rows", None),
        P("rows", "cols"),
        P("rows", "cols"),
        P("cols", "rows"),
        P("cols", "rows"),
        P("rows", "cols"),
        P(),
        P("rows", "cols"),
        P("rows", "cols"),
    )
    out_specs = (
        P("rows", "cols"),
        P(),
        P("rows", "cols"),
        P("cols"),
        P("cols"),
        P("rows", "cols"),
        P("rows", "cols"),
        P("rows", None),
        P("rows", "cols"),
        P("rows", "cols"),
        P("cols", "rows"),
        P("cols", "rows"),
        P("rows", "cols"),
        P("rows", "cols"),
        P("rows", "cols"),
        P("rows", None),
        P("rows", "cols"),
        P("rows", "cols"),
        P("cols", "rows"),
        P("cols", "rows"),
        P("rows", "cols"),
    )
    return jax.shard_map(shards, mesh=mesh, in_specs=in_specs, out_specs=out_specs, check_vma=False)
```

```python
import jax
import jax.numpy as jnp
from jax import lax
from jax.sharding import PartitionSpec as P

NORM_EPS = 1e-06
BF = jnp.bfloat16
F32 = jnp.float32


def product(former, latter):
    return jnp.dot(former, latter, preferred_element_type=F32)


def left_trans(former, latter):
    return lax.dot_general(
        former, latter, (((0,), (0,)), ((), ())), preferred_element_type=F32
    )


def right_trans(former, latter):
    return lax.dot_general(
        former, latter, (((1,), (1,)), ((), ())), preferred_element_type=F32
    )


def angles(length, head_size):
    half_size = head_size // 2
    inverse = 10000.0 ** (-(jnp.arange(half_size, dtype=F32) * 2.0 / head_size))
    theta = jnp.arange(length, dtype=F32)[:, None] * inverse[None, :]
    return (jnp.cos(theta), jnp.sin(theta))


def rotate(values_in, cosine_table, sine_table):
    half_size = values_in.shape[-1] // 2
    first_half = values_in[..., :half_size]
    second_half = values_in[..., half_size:]
    return jnp.concatenate(
        [
            first_half * cosine_table - second_half * sine_table,
            second_half * cosine_table + first_half * sine_table,
        ],
        axis=-1,
    )


def allowed_mask(key_count, length):
    row_place = jnp.arange(key_count)[:, None]
    col_place = jnp.arange(key_count)[None, :]
    return ((col_place <= row_place) & (col_place < length))[None]


def attend_forward(query_rows, key_rows, value_rows, length):
    allowed = allowed_mask(key_rows.shape[0], length)
    scores = jnp.einsum("hqd,kd->hqk", query_rows, key_rows, preferred_element_type=F32)
    masked = jnp.where(allowed, scores, -1e30)
    largest = jnp.max(masked, axis=-1, keepdims=True)
    exponent = jnp.exp(masked - largest)
    totals = jnp.sum(exponent, axis=-1, keepdims=True)
    probability = (exponent / totals).astype(BF)
    attended = jnp.einsum("hqk,kd->hqd", probability, value_rows, preferred_element_type=F32)
    return (attended.astype(BF), (largest + jnp.log(totals))[..., 0])


def attend_backward(query_rows, key_rows, value_rows, length, log_total, grad_out):
    allowed = allowed_mask(key_rows.shape[0], length)
    scores = jnp.einsum("hqd,kd->hqk", query_rows, key_rows, preferred_element_type=F32)
    probability = jnp.where(allowed, jnp.exp(scores - log_total[..., None]), 0.0)
    grad_prob = jnp.einsum("hqd,kd->hqk", grad_out, value_rows, preferred_element_type=F32)
    row_terms = jnp.sum(probability * grad_prob, axis=-1, keepdims=True)
    grad_scores = (probability * (grad_prob - row_terms)).astype(BF)
    grad_query = jnp.einsum("hqk,kd->hqd", grad_scores, key_rows, preferred_element_type=F32)
    grad_key = jnp.einsum("hqk,hqd->kd", grad_scores, query_rows, preferred_element_type=F32)
    grad_value = jnp.einsum(
        "hqk,hqd->kd", probability.astype(BF), grad_out, preferred_element_type=F32
    )
    return (grad_query, grad_key, grad_value)


def norm_scale(values_in):
    return lax.rsqrt(jnp.mean(values_in * values_in, axis=-1, keepdims=True) + NORM_EPS)


def norm_forward(values_in, gain_row):
    row_scale = norm_scale(values_in)
    return ((values_in * row_scale * (1.0 + gain_row)).astype(BF), row_scale)


def norm_backward(grad_rows, rows_in, gain_row, row_scale):
    factor = 1.0 + gain_row
    row_dots = jnp.sum(grad_rows * factor * rows_in, axis=-1, keepdims=True)
    grad_input = (
        row_scale * factor * grad_rows
        - rows_in * (row_scale * row_scale * row_scale) * row_dots / rows_in.shape[1]
    )
    return (grad_input, jnp.sum(grad_rows * rows_in * row_scale, axis=0))


def geglu(gate_lin, up_lin):
    return jax.nn.gelu(gate_lin, approximate=True) * up_lin


def solution(mesh):
    row_devices = mesh.shape["rows"]
    col_devices = mesh.shape["cols"]
    nk = 2
    nx = col_devices // nk
    nz = 4 if row_devices % 4 == 0 else row_devices
    ny = row_devices // nz
    BOTH = ("rows", "cols")

    def permute(value, move):
        pairs = []
        for z in range(nz):
            for y in range(ny):
                for x in range(nx):
                    for k in range(nk):
                        tz, ty, tx, tk = move(z, y, x, k)
                        source = (z * ny + y) * col_devices + x * nk + k
                        target = (tz * ny + ty) * col_devices + tx * nk + tk
                        pairs.append((source, target))
        return lax.ppermute(value, BOTH, pairs)

    def swap_z(value, mask):
        return permute(value, lambda z, y, x, k: (z ^ mask, y, x, k))

    def swap_y(value, mask):
        return permute(value, lambda z, y, x, k: (z, y ^ mask, x, k))

    def swap_x(value, mask):
        return permute(value, lambda z, y, x, k: (z, y, x ^ mask, k))

    def swap_k(value):
        return permute(value, lambda z, y, x, k: (z, y, x, k ^ 1))

    def ring(value):
        return permute(
            value, lambda z, y, x, k: ((z + 1) % nz if k == 0 else (z - 1) % nz, y, x, k)
        )

    def natural(parts, place):
        count = len(parts)
        arrays = list(parts)
        bit = 1
        while bit < count:
            hot = (place & bit) != 0
            arrays = [
                jnp.where(hot, arrays[slot ^ bit], arrays[slot]) for slot in range(count)
            ]
            bit *= 2
        return arrays

    def gather_cols(value, place):
        parts = [None] * col_devices
        for mask in range(nx):
            near = value if mask == 0 else swap_x(value, mask)
            parts[mask * nk] = near
            parts[mask * nk + 1] = swap_k(near)
        return natural(parts, place)

    def scatter_rest(kept, place_x):
        near = lax.dynamic_index_in_dim(kept, place_x, 0, keepdims=False)
        for mask in range(1, nx):
            away = lax.dynamic_index_in_dim(kept, place_x ^ mask, 0, keepdims=False)
            near = near + swap_x(away.astype(BF), mask).astype(F32)
        return near

    def scatter_cols(blocks, place_x, place_k, make):
        hot = place_k == 0
        away = jnp.where(hot, blocks[:, 1], blocks[:, 0])
        near = jnp.where(hot, blocks[:, 0], blocks[:, 1])
        got = swap_k(make(away).astype(BF))
        kept = make(near) + got.astype(F32)
        return scatter_rest(kept, place_x)

    def row_parts(value):
        parts = []
        for mask_z in range(nz):
            near = value if mask_z == 0 else swap_z(value, mask_z)
            parts.append(near)
            parts.extend(swap_y(near, mask) for mask in range(1, ny))
        return parts

    def scatter_y(blocks, place_y):
        blocks = blocks.reshape(nz, ny, *blocks.shape[1:])
        kept = lax.dynamic_index_in_dim(blocks, place_y, 1, keepdims=False)
        got = []
        for mask in range(1, ny):
            away = lax.dynamic_index_in_dim(blocks, place_y ^ mask, 1, keepdims=False)
            got.append(swap_y(away, mask))
        return [kept] + got

    def scatter_z(parts, place_z):
        kept = sum(part.astype(F32) for part in parts)
        got = [lax.dynamic_index_in_dim(kept, place_z, 0, keepdims=False)]
        for mask in range(1, nz):
            away = lax.dynamic_index_in_dim(kept, place_z ^ mask, 0, keepdims=False)
            got.append(swap_z(away.astype(BF), mask))
        return got

    def total(parts):
        return sum(part.astype(F32) for part in parts)

    def sum_all(value):
        for mask_count, swap in ((nz, swap_z), (ny, swap_y), (nx, swap_x)):
            bit = 1
            while bit < mask_count:
                value = value + swap(value, bit)
                bit *= 2
        return value + swap_k(value)

    def after(value, *others):
        return lax.optimization_barrier((value, *others))[0]

    def spread_x(own):
        return [own] + [swap_x(own, mask) for mask in range(1, nx)]

    def exchange(value, axis):
        return lax.all_to_all(value, axis, 0, 0, tiled=True)

    def shards(
        tokens,
        gain_attn,
        gain_mlp,
        w_q,
        w_kv,
        a_qkv,
        b_q,
        b_kv,
        w_o,
        a_o,
        b_o,
        w_gate,
        w_up,
        a_gu,
        b_gate,
        b_up,
        w_down,
        a_down,
        b_down,
        lengths,
        teacher,
        out_grad,
    ):
        row_place = lax.axis_index("rows")
        col_place = lax.axis_index("cols")
        place_x = col_place // nk
        place_z = row_place // ny
        place_y = row_place % ny
        place_k = col_place % nk
        row_count, local_features = tokens.shape
        features = local_features * col_devices
        seq_len = row_count * row_devices // lengths.shape[0]
        seqs_here = row_count // seq_len
        own_rows = row_count // col_devices
        rank = a_qkv.shape[1]
        block_d = w_q.shape[0]
        block_r = b_q.shape[0]
        block_e = block_d + block_r
        q_width = w_q.shape[1]
        kv_width = w_kv.shape[1]
        head_size = kv_width * col_devices // 2
        heads_here = q_width // head_size
        hidden_part = w_gate.shape[1] // row_devices
        lens_here = lax.dynamic_slice_in_dim(lengths, row_place * seqs_here, seqs_here)

        gain_rows = jnp.concatenate(
            [gain_attn[None], gain_mlp[None], jnp.zeros((14, local_features), BF)], axis=0
        )
        gain_full = jnp.concatenate(gather_cols(gain_rows, col_place), axis=1).astype(F32)
        gain_one = gain_full[0:1]
        gain_two = gain_full[1:2]
        full_x = jnp.concatenate(gather_cols(tokens, col_place), axis=1)

        pack_one = jnp.concatenate(
            [
                jnp.concatenate([w_q, w_kv, a_qkv], axis=1),
                jnp.concatenate([b_q, b_kv, jnp.zeros((block_r, rank), BF)], axis=1),
            ],
            axis=0,
        )
        got_one = jnp.stack(natural(row_parts(pack_one), row_place))
        slice_r = rank // col_devices
        own_a_gu = lax.dynamic_slice_in_dim(a_gu, col_place * slice_r, slice_r, 1)
        wide = lax.all_gather(
            jnp.concatenate([b_o, b_down, own_a_gu.reshape(-1, local_features)], axis=0),
            BOTH,
            axis=0,
            tiled=False,
        )

        def hidden_blocks(value):
            blocks = value.reshape(value.shape[0], row_devices, hidden_part)
            return blocks.transpose(1, 0, 2)

        def hidden_slice(value):
            return exchange(value, "rows").reshape(features, hidden_part)

        side_blocks = jnp.stack(
            [hidden_blocks(b_gate), hidden_blocks(b_up), hidden_blocks(a_down.T)], axis=1
        )
        normed, scale_one = norm_forward(full_x.astype(F32), gain_one)
        gate_own = hidden_slice(hidden_blocks(w_gate))
        pack_two = jnp.concatenate([w_o.T, a_o.T], axis=0)
        pack_two, side_blocks, gate_own, got_one = lax.optimization_barrier(
            (pack_two, side_blocks, gate_own, got_one)
        )
        parts_two = row_parts(pack_two)
        gate_parts = spread_x(gate_own)
        side_own = exchange(side_blocks, "rows")
        full_a_qkv = got_one[:, :block_d, q_width + kv_width :].reshape(features, rank)
        qkv_base = got_one[:, :block_d, : q_width + kv_width].reshape(
            features, q_width + kv_width
        )
        full_b_qkv = got_one[:, block_d:, : q_width + kv_width].reshape(rank, q_width + kv_width)
        w_qkv = (qkv_base.astype(F32) + product(full_a_qkv, full_b_qkv)).astype(BF)

        kv_piece = product(normed, w_qkv[:, q_width:])
        kv_parts = gather_cols(kv_piece, col_place)
        q_lin = product(normed, w_qkv[:, :q_width])
        kv_lin = jnp.concatenate(kv_parts, axis=1)
        up_blocks, side_own, q_lin = lax.optimization_barrier(
            (hidden_blocks(w_up), side_own, q_lin)
        )
        up_own = hidden_slice(up_blocks)
        side_parts = spread_x(side_own.transpose(1, 0, 2, 3).reshape(3, rank, hidden_part))
        query_scale = head_size ** (-0.5)
        cosine_table, sine_table = angles(seq_len, head_size)
        queries = q_lin.reshape(seqs_here, seq_len, heads_here, head_size).transpose(0, 2, 1, 3)
        queries = (rotate(queries, cosine_table, sine_table) * query_scale).astype(BF)
        keys = rotate(
            kv_lin[:, :head_size].reshape(seqs_here, seq_len, head_size),
            cosine_table,
            sine_table,
        ).astype(BF)
        values = kv_lin[:, head_size:].reshape(seqs_here, seq_len, head_size).astype(BF)
        forward_parts = [
            attend_forward(queries[s], keys[s], values[s], lens_here[s])
            for s in range(seqs_here)
        ]
        attn_rows = jnp.concatenate(
            [part[0].transpose(1, 0, 2).reshape(seq_len, q_width) for part in forward_parts],
            axis=0,
        )
        attn_rows, up_own, gate_parts, side_parts, wide, *parts_two = lax.optimization_barrier(
            (attn_rows, up_own, gate_parts, side_parts, wide, *parts_two)
        )
        up_parts = spread_x(up_own)
        down_blocks, up_own = lax.optimization_barrier((hidden_blocks(w_down.T), up_own))
        down_own = hidden_slice(down_blocks)
        got_two = jnp.stack(natural(parts_two, row_place))
        o_base = got_two[:, :block_d].reshape(features, q_width)
        full_a_o_t = got_two[:, block_d:block_e].reshape(rank, q_width)
        wide = wide.reshape(row_devices, col_devices, -1, local_features)

        def whole_b(start):
            value = wide[:, :, start : start + block_r]
            return value.transpose(0, 2, 1, 3).reshape(rank, features)

        full_b_o = whole_b(0)
        w_o_t = (o_base.astype(F32) + left_trans(full_b_o, full_a_o_t)).astype(BF)

        def scatter_tokens(rows, weight):
            blocks = rows.reshape(nx, nk, own_rows, rows.shape[1])
            hot = place_k == 0

            def partial_sum(first, second):
                block = jnp.where(hot, blocks[:, first], blocks[:, second])
                return right_trans(block.reshape(nx * own_rows, rows.shape[1]), weight)

            kept = swap_k(partial_sum(1, 0).astype(BF)).astype(F32) + partial_sum(0, 1)
            kept = kept.reshape(nx, own_rows, features)
            sent = [
                lax.dynamic_index_in_dim(kept, place_x ^ mask, 0, keepdims=False).astype(BF)
                for mask in range(1, nx)
            ]
            return (lax.dynamic_index_in_dim(kept, place_x, 0, keepdims=False), sent)

        def finish_tokens(near, sent):
            return near + total([swap_x(value, i + 1) for i, value in enumerate(sent)])

        near_one, sent_one = scatter_tokens(attn_rows, w_o_t)
        branch_one = finish_tokens(near_one, sent_one)
        own_x = lax.dynamic_slice_in_dim(full_x, col_place * own_rows, own_rows, 0).astype(F32)
        own_scale = lax.dynamic_slice_in_dim(scale_one, col_place * own_rows, own_rows, 0)
        middle = own_x + branch_one
        down_own, middle = lax.optimization_barrier((down_own, middle))
        full_b_down = whole_b(block_r)
        full_b_down_t = full_b_down.T
        full_a_gu = wide[:, :, 2 * block_r :].reshape(row_devices, col_devices, block_d, slice_r)
        full_a_gu = full_a_gu.transpose(0, 2, 1, 3).reshape(features, rank)
        gate_sides = [part[0] for part in side_parts]
        up_sides = [part[1] for part in side_parts]
        down_sides = [part[2] for part in side_parts]

        def joined(bases, sides, factor):
            parts = [
                (base.astype(F32) + product(factor, side)).astype(BF)
                for base, side in zip(bases, sides)
            ]
            return jnp.concatenate(parts, axis=1)

        middle_low = middle.astype(BF).astype(F32)
        normed_two, scale_two = norm_forward(middle_low, gain_two)

        def gather_ring(value, work):
            chunks = []
            for step in range(nz):
                lines = [swap_y(value, mask) for mask in range(1, ny)]
                near = value
                if step + 1 < nz:
                    value = ring(value)
                    if step:
                        lines, value = lax.optimization_barrier((lines, value))
                    else:
                        chunks.append(jnp.concatenate([near, swap_k(near)], axis=0))
                        lines, value, done = lax.optimization_barrier(
                            (lines, value, work(chunks[0]))
                        )
                for line in ([near] if step else []) + lines:
                    chunks.append(jnp.concatenate([line, swap_k(line)], axis=0))
            return (chunks, done)

        def scatter_ring(parts, extra=None):
            totals = []
            for step in list(range(1, nz)) + [0]:
                mine = None
                for mask in reversed(range(ny)):
                    part = parts[step * ny + mask]
                    away = swap_k(part[own_rows:].astype(BF))
                    chip = part[:own_rows] + away.astype(F32)
                    if mask:
                        chip = swap_y(chip.astype(BF), mask).astype(F32)
                    mine = chip if mine is None else mine + chip
                if step == 0 and extra is not None:
                    totals[-1], extra = lax.optimization_barrier((totals[-1], extra))
                if totals:
                    mine = mine + ring(totals[-1]).astype(F32)
                totals.append(mine.astype(BF) if step else mine)
            return (totals, extra)

        normed_chunks, normed_two = gather_ring(normed_two, lambda chunk: chunk)
        up_parts, normed_chunks[1] = lax.optimization_barrier((up_parts, normed_chunks[1]))
        gate_w = joined(gate_parts, gate_sides, full_a_gu)
        up_w = joined(up_parts, up_sides, full_a_gu)
        down_parts = spread_x(down_own)
        down_parts, normed_chunks[-ny] = lax.optimization_barrier(
            (down_parts, normed_chunks[-ny])
        )
        down_w = joined(down_parts, down_sides, full_b_down_t)
        pair = jnp.stack([teacher, out_grad]).reshape(
            2, col_devices, own_rows, local_features
        )
        pair = exchange(after(pair.transpose(1, 0, 2, 3), down_own), "cols")
        gates, ups, hiddens, parts = [], [], [], []
        for chunk in normed_chunks:
            gate_lin = product(chunk, gate_w)
            up_lin = product(chunk, up_w)
            hidden = geglu(gate_lin, up_lin).astype(BF)
            gates.append(gate_lin)
            ups.append(up_lin)
            hiddens.append(hidden)
            parts.append(right_trans(hidden, down_w))
        pair, parts[0] = lax.optimization_barrier((pair, parts[0]))
        pair = pair.transpose(1, 2, 0, 3).reshape(2, own_rows, features)
        teacher_own = pair[0].astype(F32)
        out_grad_own = pair[1].astype(F32)
        result = middle + scatter_ring(parts)[0][-1]

        spots = col_place * own_rows + jnp.arange(own_rows)
        limits = jnp.take(lens_here, spots // seq_len) if seqs_here > 1 else lens_here[0]
        valid_rows = ((spots % seq_len) < limits).astype(F32)[:, None]
        valid_count = jnp.sum(lengths).astype(F32)
        error_rows = result - teacher_own
        square = jnp.sum(error_rows * error_rows * valid_rows)
        total_tokens = row_count * row_devices
        seed_grad = out_grad_own + total_tokens / valid_count * error_rows * valid_rows
        grad_two = seed_grad.astype(BF)

        def to_columns(value):
            blocks = value.reshape(own_rows, col_devices, local_features).transpose(1, 0, 2)
            parts = []
            for mask in range(col_devices):
                block = lax.dynamic_index_in_dim(blocks, col_place ^ mask, 0, keepdims=False)
                if mask:
                    block = permute(
                        block,
                        lambda z, y, x, k, mask=mask: (z, y, x ^ (mask // nk), k ^ (mask % nk)),
                    )
                parts.append(block)
            return jnp.concatenate(natural(parts, col_place), axis=0)


        grad_chunks, first_hidden = gather_ring(
            grad_two, lambda chunk: product(chunk, down_w)
        )
        d_gates, d_ups, parts = [], [], []
        for chunk, gate_lin, up_lin in zip(grad_chunks, gates, ups):
            d_hidden = product(chunk, down_w) if d_gates else first_hidden
            _, geglu_back = jax.vjp(geglu, gate_lin, up_lin)
            d_gate, d_up = geglu_back(d_hidden)
            d_gate = d_gate.astype(BF)
            d_up = d_up.astype(BF)
            d_gates.append(d_gate)
            d_ups.append(d_up)
            parts.append(right_trans(d_gate, gate_w) + right_trans(d_up, up_w))
        totals, normed_all = scatter_ring(parts, jnp.concatenate(normed_chunks, axis=0))
        d_normed_two = totals[-1]

        def weight_grad(left, right, factor, i):
            piece = right[:, i * hidden_part : (i + 1) * hidden_part]
            whole = left_trans(left, piece).astype(BF)
            side = left_trans(factor, whole).astype(BF)
            pack = jnp.concatenate(
                [
                    whole.reshape(row_devices, block_d, hidden_part),
                    side.reshape(row_devices, block_r, hidden_part),
                ],
                axis=1,
            )
            return (pack, whole)

        def weight_grads(left, right, factor):
            pairs = [weight_grad(left, right, factor, i) for i in range(nx)]
            return ([pair[0] for pair in pairs], [pair[1] for pair in pairs])

        def share_x(packs):
            return [swap_x(packs[mask], mask) for mask in range(1, nx)]

        def owned(kept, got):
            return exchange(total([kept] + got).astype(BF), "rows")

        def in_place(own):
            block = jnp.concatenate([own[r] for r in range(row_devices)], axis=1)
            return (block[:block_d].astype(F32), block[block_d:].astype(F32))

        def inner(sides, wholes):
            return sum(right_trans(side, whole) for side, whole in zip(sides, wholes))

        grad_all = after(jnp.concatenate(grad_chunks, axis=0), parts[-1])
        down_packs, down_all = weight_grads(
            grad_all, jnp.concatenate(hiddens, axis=0), full_b_down_t
        )
        down_got = share_x(down_packs)
        d_norm_two, gain_two_part = norm_backward(d_normed_two, middle_low, gain_two, scale_two)
        d_middle = seed_grad + d_norm_two

        grad_one = d_middle.astype(BF)
        near_parts = spread_x(grad_one)
        gates_all = jnp.concatenate(d_gates, axis=0)
        gate_away = [
            weight_grad(normed_all, gates_all, full_a_gu, i) for i in range(1, nx)
        ]
        gate_away, near_parts, down_got, normed_all = lax.optimization_barrier(
            (gate_away, near_parts, down_got, normed_all)
        )
        gate_got = [swap_x(pair[0], i + 1) for i, pair in enumerate(gate_away)]
        ups_all = jnp.concatenate(d_ups, axis=0)
        up_away = [weight_grad(normed_all, ups_all, full_a_gu, i) for i in range(1, nx)]
        up_away, gate_got, normed_all = lax.optimization_barrier((up_away, gate_got, normed_all))
        up_got = [swap_x(pair[0], i + 1) for i, pair in enumerate(up_away)]
        gate_near = weight_grad(normed_all, gates_all, full_a_gu, 0)
        gate_all = [pair[1] for pair in [gate_near] + gate_away]
        up_near = weight_grad(normed_all, ups_all, full_a_gu, 0)
        up_all = [pair[1] for pair in [up_near] + up_away]
        down_g = owned(down_packs[0], down_got)
        grad_parts = []
        for near in near_parts:
            grad_parts.extend([near, swap_k(near)])
        grad_one_full = jnp.concatenate(natural(grad_parts, col_place), axis=0)
        d_attended = product(grad_one_full, w_o_t).astype(BF)
        down_g, d_attended = lax.optimization_barrier((down_g, d_attended))
        gate_mine, down_g = lax.optimization_barrier((gate_near[0], down_g))
        gate_g = owned(gate_mine, gate_got)
        d_heads = d_attended.reshape(seqs_here, seq_len, heads_here, head_size)
        d_heads = d_heads.transpose(0, 2, 1, 3)
        q_pieces, kv_pieces = [], []
        for s in range(seqs_here):
            d_query, d_key, d_value = attend_backward(
                queries[s], keys[s], values[s], lens_here[s], forward_parts[s][1], d_heads[s]
            )
            d_query = rotate(d_query * query_scale, cosine_table, -sine_table)
            q_pieces.append(d_query.transpose(1, 0, 2).reshape(seq_len, q_width).astype(BF))
            d_key = rotate(d_key, cosine_table, -sine_table)
            kv_pieces.append(jnp.concatenate([d_key, d_value], axis=1))
        d_q_lin = jnp.concatenate(q_pieces, axis=0)
        up_got, gate_g, d_q_lin = lax.optimization_barrier((up_got, gate_g, d_q_lin))
        up_g = owned(up_near[0], up_got)
        kv_blocks = jnp.concatenate(kv_pieces, axis=0).reshape(row_count, nx, nk, kv_width)
        d_kv_lin = scatter_cols(
            kv_blocks.transpose(1, 2, 0, 3), place_x, place_k, lambda block: block
        ).astype(BF)
        d_qkv = jnp.concatenate([d_q_lin, d_kv_lin], axis=1)
        near_two, sent = scatter_tokens(d_qkv, w_qkv)
        up_g, sent = lax.optimization_barrier((up_g, sent))
        d_normed = finish_tokens(near_two, sent)

        def blocks_of(value):
            return value.reshape(value.shape[0], nx, nk, -1).transpose(1, 2, 0, 3)

        def rank_blocks(value):
            blocks = value.reshape(nx, nk, slice_r, row_devices, block_d)
            blocks = blocks.transpose(0, 1, 3, 2, 4)
            return blocks.reshape(nx, nk, rank, local_features)

        o_rows = after(grad_one_full, d_kv_lin)
        o_grad_t = left_trans(o_rows, attn_rows).astype(BF)
        a_o_grad_t = product(full_b_o, o_grad_t).astype(BF)
        shared = jnp.concatenate(
            [
                blocks_of(right_trans(full_a_o_t, o_grad_t)),
                blocks_of(inner(down_sides, down_all)),
                rank_blocks(
                    inner(gate_sides, gate_all) + inner(up_sides, up_all)
                ),
            ],
            axis=2,
        )
        shared = scatter_cols(shared, place_x, place_k, lambda block: block).astype(BF)
        shared = shared.reshape(3, row_devices, block_r, local_features).transpose(1, 0, 2, 3)
        o_parts = scatter_y(
            jnp.concatenate(
                [
                    o_grad_t.reshape(row_devices, block_d, q_width),
                    a_o_grad_t.reshape(row_devices, block_r, q_width),
                    shared.reshape(row_devices, 3 * block_r, local_features),
                ],
                axis=1,
            ),
            place_y,
        )
        qkv_grad = left_trans(normed, d_qkv).astype(BF)
        b_qkv_grad = left_trans(full_a_qkv, qkv_grad).astype(BF)
        a_qkv_part = rank_blocks(right_trans(full_b_qkv, qkv_grad))
        a_qkv_part = scatter_cols(a_qkv_part, place_x, place_k, lambda block: block).astype(BF)
        rank_parts = scatter_y(a_qkv_part.reshape(row_devices, block_r, local_features), place_y)
        last_parts = scatter_y(
            jnp.concatenate(
                [
                    qkv_grad.reshape(row_devices, -1, kv_width),
                    b_qkv_grad.reshape(row_devices, -1, kv_width),
                    ],
                axis=1,
            ),
            place_y,
        )
        last_parts, d_normed = lax.optimization_barrier((last_parts, d_normed))
        last_parts = scatter_z(last_parts, place_z)
        rank_parts = scatter_z(rank_parts, place_z)
        d_norm_one, gain_one_part = norm_backward(d_normed, own_x, gain_one, own_scale)
        grad_low_x = (d_middle + d_norm_one).astype(BF)
        o_parts = scatter_z(o_parts, place_z)
        o_parts, grad_low_x = lax.optimization_barrier((o_parts, grad_low_x))
        result_low, grad_low_x = lax.optimization_barrier((result.astype(BF), grad_low_x))
        grad_tokens = to_columns(grad_low_x).astype(F32)
        output = to_columns(result_low)
        vectors = jnp.concatenate(
            [
                gain_one_part[None],
                gain_two_part[None],
                jnp.full((1, features), square, F32),
            ],
            axis=0,
        )
        sums = sum_all(vectors)
        last_parts, rank_parts, sums = lax.optimization_barrier((last_parts, rank_parts, sums))
        down_g, d_down_side = in_place(down_g)
        gate_g, d_gate_side = in_place(gate_g)
        up_g, d_up_side = in_place(up_g)

        def join_ranks(value):
            value = value.reshape(slice_r, block_d).astype(BF)
            return jnp.concatenate(gather_cols(value, col_place), axis=0).T.astype(F32)

        rows_sum = total(o_parts)
        grad_w_o = rows_sum[:block_d].T
        grad_a_o = rows_sum[block_d:block_e].T
        grad_b_o = rows_sum[block_e : block_e + block_r]
        grad_b_down = rows_sum[block_e + block_r : block_e + 2 * block_r]
        a_gu_own = rows_sum[block_e + 2 * block_r :]
        last_sum = total(last_parts)
        wide_q = q_width + kv_width
        first_cut = block_d * wide_q // kv_width
        grad_w_qkv = last_sum[:first_cut].reshape(block_d, wide_q)
        grad_b_qkv = last_sum[first_cut:].reshape(block_r, wide_q)
        a_qkv_own = total(rank_parts)
        grad_a_gu = join_ranks(a_gu_own)
        grad_a_qkv = join_ranks(a_qkv_own)
        grad_w_q = grad_w_qkv[:, :q_width]
        grad_w_kv = grad_w_qkv[:, q_width:]
        grad_b_q = grad_b_qkv[:, :q_width]
        grad_b_kv = grad_b_qkv[:, q_width:]
        gains = lax.dynamic_slice_in_dim(sums, col_place * local_features, local_features, 1)
        loss_value = (sums[2, 0] / (2.0 * valid_count)).reshape(1)
        return (
            output,
            loss_value,
            grad_tokens,
            gains[0],
            gains[1],
            grad_w_q,
            grad_w_kv,
            grad_a_qkv,
            grad_b_q,
            grad_b_kv,
            grad_w_o,
            grad_a_o,
            grad_b_o,
            gate_g,
            up_g,
            grad_a_gu,
            d_gate_side,
            d_up_side,
            down_g.T,
            d_down_side.T,
            grad_b_down,
        )

    in_specs = (
        P("rows", "cols"),
        P("cols"),
        P("cols"),
        P("rows", "cols"),
        P("rows", "cols"),
        P("rows", None),
        P("rows", "cols"),
        P("rows", "cols"),
        P("cols", "rows"),
        P("cols", "rows"),
        P("rows", "cols"),
        P("rows", "cols"),
        P("rows", "cols"),
        P("rows", None),
        P("rows", "cols"),
        P("rows", "cols"),
        P("cols", "rows"),
        P("cols", "rows"),
        P("rows", "cols"),
        P(),
        P("rows", "cols"),
        P("rows", "cols"),
    )
    out_specs = (
        P("rows", "cols"),
        P(),
        P("rows", "cols"),
        P("cols"),
        P("cols"),
        P("rows", "cols"),
        P("rows", "cols"),
        P("rows", None),
        P("rows", "cols"),
        P("rows", "cols"),
        P("cols", "rows"),
        P("cols", "rows"),
        P("rows", "cols"),
        P("rows", "cols"),
        P("rows", "cols"),
        P("rows", None),
        P("rows", "cols"),
        P("rows", "cols"),
        P("cols", "rows"),
        P("cols", "rows"),
        P("rows", "cols"),
    )
    return jax.shard_map(shards, mesh=mesh, in_specs=in_specs, out_specs=out_specs, check_vma=False)
```

```python
import jax
import jax.numpy as jnp
from jax import lax
from jax.sharding import PartitionSpec as P

NORM_EPS = 1e-06
BF = jnp.bfloat16
F32 = jnp.float32


def product(former, latter):
    return jnp.dot(former, latter, preferred_element_type=F32)


def left_trans(former, latter):
    return lax.dot_general(
        former, latter, (((0,), (0,)), ((), ())), preferred_element_type=F32
    )


def right_trans(former, latter):
    return lax.dot_general(
        former, latter, (((1,), (1,)), ((), ())), preferred_element_type=F32
    )


def angles(length, head_size):
    half_size = head_size // 2
    inverse = 10000.0 ** (-(jnp.arange(half_size, dtype=F32) * 2.0 / head_size))
    theta = jnp.arange(length, dtype=F32)[:, None] * inverse[None, :]
    return (jnp.cos(theta), jnp.sin(theta))


def rotate(values_in, cosine_table, sine_table):
    half_size = values_in.shape[-1] // 2
    first_half = values_in[..., :half_size]
    second_half = values_in[..., half_size:]
    return jnp.concatenate(
        [
            first_half * cosine_table - second_half * sine_table,
            second_half * cosine_table + first_half * sine_table,
        ],
        axis=-1,
    )


def allowed_mask(key_count, length):
    row_place = jnp.arange(key_count)[:, None]
    col_place = jnp.arange(key_count)[None, :]
    return ((col_place <= row_place) & (col_place < length))[None]


def attend_forward(query_rows, key_rows, value_rows, length):
    allowed = allowed_mask(key_rows.shape[0], length)
    scores = jnp.einsum("hqd,kd->hqk", query_rows, key_rows, preferred_element_type=F32)
    masked = jnp.where(allowed, scores, -1e30)
    largest = jnp.max(masked, axis=-1, keepdims=True)
    exponent = jnp.exp(masked - largest)
    totals = jnp.sum(exponent, axis=-1, keepdims=True)
    probability = (exponent / totals).astype(BF)
    attended = jnp.einsum("hqk,kd->hqd", probability, value_rows, preferred_element_type=F32)
    return (attended.astype(BF), (largest + jnp.log(totals))[..., 0])


def attend_backward(query_rows, key_rows, value_rows, length, log_total, grad_out):
    allowed = allowed_mask(key_rows.shape[0], length)
    scores = jnp.einsum("hqd,kd->hqk", query_rows, key_rows, preferred_element_type=F32)
    probability = jnp.where(allowed, jnp.exp(scores - log_total[..., None]), 0.0)
    grad_prob = jnp.einsum("hqd,kd->hqk", grad_out, value_rows, preferred_element_type=F32)
    row_terms = jnp.sum(probability * grad_prob, axis=-1, keepdims=True)
    grad_scores = (probability * (grad_prob - row_terms)).astype(BF)
    grad_query = jnp.einsum("hqk,kd->hqd", grad_scores, key_rows, preferred_element_type=F32)
    grad_key = jnp.einsum("hqk,hqd->kd", grad_scores, query_rows, preferred_element_type=F32)
    grad_value = jnp.einsum(
        "hqk,hqd->kd", probability.astype(BF), grad_out, preferred_element_type=F32
    )
    return (grad_query, grad_key, grad_value)


def norm_scale(values_in):
    return lax.rsqrt(jnp.mean(values_in * values_in, axis=-1, keepdims=True) + NORM_EPS)


def norm_forward(values_in, gain_row):
    row_scale = norm_scale(values_in)
    return ((values_in * row_scale * (1.0 + gain_row)).astype(BF), row_scale)


def norm_backward(grad_rows, rows_in, gain_row, row_scale):
    factor = 1.0 + gain_row
    row_dots = jnp.sum(grad_rows * factor * rows_in, axis=-1, keepdims=True)
    grad_input = (
        row_scale * factor * grad_rows
        - rows_in * (row_scale * row_scale * row_scale) * row_dots / rows_in.shape[1]
    )
    return (grad_input, jnp.sum(grad_rows * rows_in * row_scale, axis=0))


def geglu(gate_lin, up_lin):
    return jax.nn.gelu(gate_lin, approximate=True) * up_lin


def solution(mesh):
    row_devices = mesh.shape["rows"]
    col_devices = mesh.shape["cols"]
    nk = 2
    nx = col_devices // nk
    nz = 4 if row_devices % 4 == 0 else row_devices
    ny = row_devices // nz
    BOTH = ("rows", "cols")

    def permute(value, move):
        pairs = []
        for z in range(nz):
            for y in range(ny):
                for x in range(nx):
                    for k in range(nk):
                        tz, ty, tx, tk = move(z, y, x, k)
                        source = (z * ny + y) * col_devices + x * nk + k
                        target = (tz * ny + ty) * col_devices + tx * nk + tk
                        pairs.append((source, target))
        return lax.ppermute(value, BOTH, pairs)

    def swap_z(value, mask):
        return permute(value, lambda z, y, x, k: (z ^ mask, y, x, k))

    def swap_y(value, mask):
        return permute(value, lambda z, y, x, k: (z, y ^ mask, x, k))

    def swap_x(value, mask):
        return permute(value, lambda z, y, x, k: (z, y, x ^ mask, k))

    def swap_k(value):
        return permute(value, lambda z, y, x, k: (z, y, x, k ^ 1))

    def ring(value):
        return permute(
            value, lambda z, y, x, k: ((z + 1) % nz if k == 0 else (z - 1) % nz, y, x, k)
        )

    def natural(parts, place):
        count = len(parts)
        arrays = list(parts)
        bit = 1
        while bit < count:
            hot = (place & bit) != 0
            arrays = [
                jnp.where(hot, arrays[slot ^ bit], arrays[slot]) for slot in range(count)
            ]
            bit *= 2
        return arrays

    def gather_cols(value, place):
        parts = [None] * col_devices
        for mask in range(nx):
            near = value if mask == 0 else swap_x(value, mask)
            parts[mask * nk] = near
            parts[mask * nk + 1] = swap_k(near)
        return natural(parts, place)

    def scatter_rest(kept, place_x):
        near = lax.dynamic_index_in_dim(kept, place_x, 0, keepdims=False)
        for mask in range(1, nx):
            away = lax.dynamic_index_in_dim(kept, place_x ^ mask, 0, keepdims=False)
            near = near + swap_x(away.astype(BF), mask).astype(F32)
        return near

    def scatter_cols(blocks, place_x, place_k, make):
        hot = place_k == 0
        away = jnp.where(hot, blocks[:, 1], blocks[:, 0])
        near = jnp.where(hot, blocks[:, 0], blocks[:, 1])
        got = swap_k(make(away).astype(BF))
        kept = make(near) + got.astype(F32)
        return scatter_rest(kept, place_x)

    def row_parts(value):
        parts = []
        for mask_z in range(nz):
            near = value if mask_z == 0 else swap_z(value, mask_z)
            parts.append(near)
            parts.extend(swap_y(near, mask) for mask in range(1, ny))
        return parts

    def scatter_y(blocks, place_y):
        blocks = blocks.reshape(nz, ny, *blocks.shape[1:])
        kept = lax.dynamic_index_in_dim(blocks, place_y, 1, keepdims=False)
        got = []
        for mask in range(1, ny):
            away = lax.dynamic_index_in_dim(blocks, place_y ^ mask, 1, keepdims=False)
            got.append(swap_y(away, mask))
        return [kept] + got

    def scatter_z(parts, place_z):
        kept = sum(part.astype(F32) for part in parts)
        got = [lax.dynamic_index_in_dim(kept, place_z, 0, keepdims=False)]
        for mask in range(1, nz):
            away = lax.dynamic_index_in_dim(kept, place_z ^ mask, 0, keepdims=False)
            got.append(swap_z(away.astype(BF), mask))
        return got

    def total(parts):
        return sum(part.astype(F32) for part in parts)

    def sum_all(value):
        for mask_count, swap in ((nz, swap_z), (ny, swap_y), (nx, swap_x)):
            bit = 1
            while bit < mask_count:
                value = value + swap(value, bit)
                bit *= 2
        return value + swap_k(value)

    def after(value, *others):
        return lax.optimization_barrier((value, *others))[0]

    def spread_x(own):
        return [own] + [swap_x(own, mask) for mask in range(1, nx)]

    def exchange(value, axis):
        return lax.all_to_all(value, axis, 0, 0, tiled=True)

    def shards(
        tokens,
        gain_attn,
        gain_mlp,
        w_q,
        w_kv,
        a_qkv,
        b_q,
        b_kv,
        w_o,
        a_o,
        b_o,
        w_gate,
        w_up,
        a_gu,
        b_gate,
        b_up,
        w_down,
        a_down,
        b_down,
        lengths,
        teacher,
        out_grad,
    ):
        row_place = lax.axis_index("rows")
        col_place = lax.axis_index("cols")
        place_x = col_place // nk
        place_z = row_place // ny
        place_y = row_place % ny
        place_k = col_place % nk
        row_count, local_features = tokens.shape
        features = local_features * col_devices
        seq_len = row_count * row_devices // lengths.shape[0]
        seqs_here = row_count // seq_len
        own_rows = row_count // col_devices
        rank = a_qkv.shape[1]
        block_d = w_q.shape[0]
        block_r = b_q.shape[0]
        block_e = block_d + block_r
        q_width = w_q.shape[1]
        kv_width = w_kv.shape[1]
        head_size = kv_width * col_devices // 2
        heads_here = q_width // head_size
        hidden_part = w_gate.shape[1] // row_devices
        lens_here = lax.dynamic_slice_in_dim(lengths, row_place * seqs_here, seqs_here)

        gain_rows = jnp.concatenate(
            [gain_attn[None], gain_mlp[None], jnp.zeros((14, local_features), BF)], axis=0
        )
        gain_full = jnp.concatenate(gather_cols(gain_rows, col_place), axis=1).astype(F32)
        gain_one = gain_full[0:1]
        gain_two = gain_full[1:2]
        full_x = jnp.concatenate(gather_cols(tokens, col_place), axis=1)

        pack_one = jnp.concatenate(
            [
                jnp.concatenate([w_q, w_kv, a_qkv], axis=1),
                jnp.concatenate([b_q, b_kv, jnp.zeros((block_r, rank), BF)], axis=1),
            ],
            axis=0,
        )
        got_one = jnp.stack(natural(row_parts(pack_one), row_place))
        slice_r = rank // col_devices
        own_a_gu = lax.dynamic_slice_in_dim(a_gu, col_place * slice_r, slice_r, 1)
        wide = lax.all_gather(
            jnp.concatenate([b_o, b_down, own_a_gu.reshape(-1, local_features)], axis=0),
            BOTH,
            axis=0,
            tiled=False,
        )

        def hidden_blocks(value):
            blocks = value.reshape(value.shape[0], row_devices, hidden_part)
            return blocks.transpose(1, 0, 2)

        def hidden_slice(value):
            return exchange(value, "rows").reshape(features, hidden_part)

        side_blocks = jnp.stack(
            [hidden_blocks(b_gate), hidden_blocks(b_up), hidden_blocks(a_down.T)], axis=1
        )
        normed, scale_one = norm_forward(full_x.astype(F32), gain_one)
        gate_own = hidden_slice(hidden_blocks(w_gate))
        pack_two = jnp.concatenate([w_o.T, a_o.T], axis=0)
        pack_two, side_blocks, gate_own, got_one = lax.optimization_barrier(
            (pack_two, side_blocks, gate_own, got_one)
        )
        parts_two = row_parts(pack_two)
        gate_parts = spread_x(gate_own)
        side_own = exchange(side_blocks, "rows")
        full_a_qkv = got_one[:, :block_d, q_width + kv_width :].reshape(features, rank)
        qkv_base = got_one[:, :block_d, : q_width + kv_width].reshape(
            features, q_width + kv_width
        )
        full_b_qkv = got_one[:, block_d:, : q_width + kv_width].reshape(rank, q_width + kv_width)
        w_qkv = (qkv_base.astype(F32) + product(full_a_qkv, full_b_qkv)).astype(BF)

        kv_piece = product(normed, w_qkv[:, q_width:])
        kv_parts = gather_cols(kv_piece, col_place)
        q_lin = product(normed, w_qkv[:, :q_width])
        kv_lin = jnp.concatenate(kv_parts, axis=1)
        up_blocks, side_own, q_lin = lax.optimization_barrier(
            (hidden_blocks(w_up), side_own, q_lin)
        )
        up_own = hidden_slice(up_blocks)
        side_parts = spread_x(side_own.transpose(1, 0, 2, 3).reshape(3, rank, hidden_part))
        query_scale = head_size ** (-0.5)
        cosine_table, sine_table = angles(seq_len, head_size)
        queries = q_lin.reshape(seqs_here, seq_len, heads_here, head_size).transpose(0, 2, 1, 3)
        queries = (rotate(queries, cosine_table, sine_table) * query_scale).astype(BF)
        keys = rotate(
            kv_lin[:, :head_size].reshape(seqs_here, seq_len, head_size),
            cosine_table,
            sine_table,
        ).astype(BF)
        values = kv_lin[:, head_size:].reshape(seqs_here, seq_len, head_size).astype(BF)
        forward_parts = [
            attend_forward(queries[s], keys[s], values[s], lens_here[s])
            for s in range(seqs_here)
        ]
        attn_rows = jnp.concatenate(
            [part[0].transpose(1, 0, 2).reshape(seq_len, q_width) for part in forward_parts],
            axis=0,
        )
        attn_rows, up_own, gate_parts, side_parts, wide, *parts_two = lax.optimization_barrier(
            (attn_rows, up_own, gate_parts, side_parts, wide, *parts_two)
        )
        up_parts = spread_x(up_own)
        down_blocks, up_own = lax.optimization_barrier((hidden_blocks(w_down.T), up_own))
        down_own = hidden_slice(down_blocks)
        got_two = jnp.stack(natural(parts_two, row_place))
        o_base = got_two[:, :block_d].reshape(features, q_width)
        full_a_o_t = got_two[:, block_d:block_e].reshape(rank, q_width)
        wide = wide.reshape(row_devices, col_devices, -1, local_features)

        def whole_b(start):
            value = wide[:, :, start : start + block_r]
            return value.transpose(0, 2, 1, 3).reshape(rank, features)

        full_b_o = whole_b(0)
        w_o_t = (o_base.astype(F32) + left_trans(full_b_o, full_a_o_t)).astype(BF)

        def scatter_tokens(rows, weight):
            blocks = rows.reshape(nx, nk, own_rows, rows.shape[1])
            hot = place_k == 0

            def partial_sum(first, second):
                block = jnp.where(hot, blocks[:, first], blocks[:, second])
                return right_trans(block.reshape(nx * own_rows, rows.shape[1]), weight)

            kept = swap_k(partial_sum(1, 0).astype(BF)).astype(F32) + partial_sum(0, 1)
            kept = kept.reshape(nx, own_rows, features)
            sent = [
                lax.dynamic_index_in_dim(kept, place_x ^ mask, 0, keepdims=False).astype(BF)
                for mask in range(1, nx)
            ]
            return (lax.dynamic_index_in_dim(kept, place_x, 0, keepdims=False), sent)

        def finish_tokens(near, sent):
            return near + total([swap_x(value, i + 1) for i, value in enumerate(sent)])

        near_one, sent_one = scatter_tokens(attn_rows, w_o_t)
        branch_one = finish_tokens(near_one, sent_one)
        own_x = lax.dynamic_slice_in_dim(full_x, col_place * own_rows, own_rows, 0).astype(F32)
        own_scale = lax.dynamic_slice_in_dim(scale_one, col_place * own_rows, own_rows, 0)
        middle = own_x + branch_one
        down_own, middle = lax.optimization_barrier((down_own, middle))
        full_b_down = whole_b(block_r)
        full_b_down_t = full_b_down.T
        full_a_gu = wide[:, :, 2 * block_r :].reshape(row_devices, col_devices, block_d, slice_r)
        full_a_gu = full_a_gu.transpose(0, 2, 1, 3).reshape(features, rank)
        gate_sides = [part[0] for part in side_parts]
        up_sides = [part[1] for part in side_parts]
        down_sides = [part[2] for part in side_parts]

        def joined(bases, sides, factor):
            parts = [
                (base.astype(F32) + product(factor, side)).astype(BF)
                for base, side in zip(bases, sides)
            ]
            return jnp.concatenate(parts, axis=1)

        middle_low = middle.astype(BF).astype(F32)
        normed_two, scale_two = norm_forward(middle_low, gain_two)

        def gather_ring(value, work):
            chunks = []
            for step in range(nz):
                lines = [swap_y(value, mask) for mask in range(1, ny)]
                near = value
                if step + 1 < nz:
                    value = ring(value)
                    if step:
                        lines, value = lax.optimization_barrier((lines, value))
                    else:
                        chunks.append(jnp.concatenate([near, swap_k(near)], axis=0))
                        lines, value, done = lax.optimization_barrier(
                            (lines, value, work(chunks[0]))
                        )
                for line in ([near] if step else []) + lines:
                    chunks.append(jnp.concatenate([line, swap_k(line)], axis=0))
            return (chunks, done)

        def scatter_ring(parts, extra=None):
            totals = []
            for step in list(range(1, nz)) + [0]:
                mine = None
                for mask in reversed(range(ny)):
                    part = parts[step * ny + mask]
                    away = swap_k(part[own_rows:].astype(BF))
                    chip = part[:own_rows] + away.astype(F32)
                    if mask:
                        chip = swap_y(chip.astype(BF), mask).astype(F32)
                    mine = chip if mine is None else mine + chip
                if step == 0 and extra is not None:
                    totals[-1], extra = lax.optimization_barrier((totals[-1], extra))
                if totals:
                    mine = mine + ring(totals[-1]).astype(F32)
                totals.append(mine.astype(BF) if step else mine)
            return (totals, extra)

        normed_chunks, normed_two = gather_ring(normed_two, lambda chunk: chunk)
        up_parts, normed_chunks[1] = lax.optimization_barrier((up_parts, normed_chunks[1]))
        gate_w = joined(gate_parts, gate_sides, full_a_gu)
        up_w = joined(up_parts, up_sides, full_a_gu)
        down_parts = spread_x(down_own)
        down_parts, normed_chunks[-ny] = lax.optimization_barrier(
            (down_parts, normed_chunks[-ny])
        )
        down_w = joined(down_parts, down_sides, full_b_down_t)
        pair = jnp.stack([teacher, out_grad]).reshape(
            2, col_devices, own_rows, local_features
        )
        pair = exchange(after(pair.transpose(1, 0, 2, 3), down_own), "cols")
        gates, ups, hiddens, parts = [], [], [], []
        for chunk in normed_chunks:
            gate_lin = product(chunk, gate_w)
            up_lin = product(chunk, up_w)
            hidden = geglu(gate_lin, up_lin).astype(BF)
            gates.append(gate_lin)
            ups.append(up_lin)
            hiddens.append(hidden)
            parts.append(right_trans(hidden, down_w))
        pair, parts[0] = lax.optimization_barrier((pair, parts[0]))
        pair = pair.transpose(1, 2, 0, 3).reshape(2, own_rows, features)
        teacher_own = pair[0].astype(F32)
        out_grad_own = pair[1].astype(F32)
        result = middle + scatter_ring(parts)[0][-1]

        spots = col_place * own_rows + jnp.arange(own_rows)
        limits = jnp.take(lens_here, spots // seq_len) if seqs_here > 1 else lens_here[0]
        valid_rows = ((spots % seq_len) < limits).astype(F32)[:, None]
        valid_count = jnp.sum(lengths).astype(F32)
        error_rows = result - teacher_own
        square = jnp.sum(error_rows * error_rows * valid_rows)
        total_tokens = row_count * row_devices
        seed_grad = out_grad_own + total_tokens / valid_count * error_rows * valid_rows
        grad_two = seed_grad.astype(BF)

        def to_columns(value):
            blocks = value.reshape(own_rows, col_devices, local_features).transpose(1, 0, 2)
            parts = []
            for mask in range(col_devices):
                block = lax.dynamic_index_in_dim(blocks, col_place ^ mask, 0, keepdims=False)
                if mask:
                    block = permute(
                        block,
                        lambda z, y, x, k, mask=mask: (z, y, x ^ (mask // nk), k ^ (mask % nk)),
                    )
                parts.append(block)
            return jnp.concatenate(natural(parts, col_place), axis=0)


        grad_chunks, first_hidden = gather_ring(
            grad_two, lambda chunk: product(chunk, down_w)
        )
        d_gates, d_ups, parts = [], [], []
        for chunk, gate_lin, up_lin in zip(grad_chunks, gates, ups):
            d_hidden = product(chunk, down_w) if d_gates else first_hidden
            _, geglu_back = jax.vjp(geglu, gate_lin, up_lin)
            d_gate, d_up = geglu_back(d_hidden)
            d_gate = d_gate.astype(BF)
            d_up = d_up.astype(BF)
            d_gates.append(d_gate)
            d_ups.append(d_up)
            parts.append(right_trans(d_gate, gate_w) + right_trans(d_up, up_w))
        totals, normed_all = scatter_ring(parts, jnp.concatenate(normed_chunks, axis=0))
        d_normed_two = totals[-1]

        def weight_grad(left, right, factor, i):
            piece = right[:, i * hidden_part : (i + 1) * hidden_part]
            whole = left_trans(left, piece).astype(BF)
            side = left_trans(factor, whole).astype(BF)
            pack = jnp.concatenate(
                [
                    whole.reshape(row_devices, block_d, hidden_part),
                    side.reshape(row_devices, block_r, hidden_part),
                ],
                axis=1,
            )
            return (pack, whole)

        def weight_grads(left, right, factor):
            pairs = [weight_grad(left, right, factor, i) for i in range(nx)]
            return ([pair[0] for pair in pairs], [pair[1] for pair in pairs])

        def share_x(packs):
            return [swap_x(packs[mask], mask) for mask in range(1, nx)]

        def owned(kept, got):
            return exchange(total([kept] + got).astype(BF), "rows")

        def in_place(own):
            block = jnp.concatenate([own[r] for r in range(row_devices)], axis=1)
            return (block[:block_d].astype(F32), block[block_d:].astype(F32))

        def inner(sides, wholes):
            return sum(right_trans(side, whole) for side, whole in zip(sides, wholes))

        grad_all = after(jnp.concatenate(grad_chunks, axis=0), parts[-1])
        down_packs, down_all = weight_grads(
            grad_all, jnp.concatenate(hiddens, axis=0), full_b_down_t
        )
        down_got = share_x(down_packs)
        d_norm_two, gain_two_part = norm_backward(d_normed_two, middle_low, gain_two, scale_two)
        d_middle = seed_grad + d_norm_two

        grad_one = d_middle.astype(BF)
        near_parts = spread_x(grad_one)
        gates_all = jnp.concatenate(d_gates, axis=0)
        gate_away = [
            weight_grad(normed_all, gates_all, full_a_gu, i) for i in range(1, nx)
        ]
        gate_away, near_parts, down_got, normed_all = lax.optimization_barrier(
            (gate_away, near_parts, down_got, normed_all)
        )
        gate_got = [swap_x(pair[0], i + 1) for i, pair in enumerate(gate_away)]
        ups_all = jnp.concatenate(d_ups, axis=0)
        up_away = [weight_grad(normed_all, ups_all, full_a_gu, i) for i in range(1, nx)]
        up_away, gate_got, normed_all = lax.optimization_barrier((up_away, gate_got, normed_all))
        up_got = [swap_x(pair[0], i + 1) for i, pair in enumerate(up_away)]
        gate_near = weight_grad(normed_all, gates_all, full_a_gu, 0)
        gate_all = [pair[1] for pair in [gate_near] + gate_away]
        up_near = weight_grad(normed_all, ups_all, full_a_gu, 0)
        up_all = [pair[1] for pair in [up_near] + up_away]
        down_g = owned(down_packs[0], down_got)
        grad_parts = []
        for near in near_parts:
            grad_parts.extend([near, swap_k(near)])
        grad_one_full = jnp.concatenate(natural(grad_parts, col_place), axis=0)
        d_attended = product(grad_one_full, w_o_t).astype(BF)
        down_g, d_attended = lax.optimization_barrier((down_g, d_attended))
        gate_mine, down_g = lax.optimization_barrier((gate_near[0], down_g))
        gate_g = owned(gate_mine, gate_got)
        d_heads = d_attended.reshape(seqs_here, seq_len, heads_here, head_size)
        d_heads = d_heads.transpose(0, 2, 1, 3)
        q_pieces, kv_pieces = [], []
        for s in range(seqs_here):
            d_query, d_key, d_value = attend_backward(
                queries[s], keys[s], values[s], lens_here[s], forward_parts[s][1], d_heads[s]
            )
            d_query = rotate(d_query * query_scale, cosine_table, -sine_table)
            q_pieces.append(d_query.transpose(1, 0, 2).reshape(seq_len, q_width).astype(BF))
            d_key = rotate(d_key, cosine_table, -sine_table)
            kv_pieces.append(jnp.concatenate([d_key, d_value], axis=1))
        d_q_lin = jnp.concatenate(q_pieces, axis=0)
        up_got, d_q_lin = lax.optimization_barrier((up_got, d_q_lin))
        kv_blocks = jnp.concatenate(kv_pieces, axis=0).reshape(row_count, nx, nk, kv_width)
        d_kv_lin = scatter_cols(
            kv_blocks.transpose(1, 2, 0, 3), place_x, place_k, lambda block: block
        ).astype(BF)
        d_qkv = jnp.concatenate([d_q_lin, d_kv_lin], axis=1)
        near_two, sent = scatter_tokens(d_qkv, w_qkv)
        gate_g, sent = lax.optimization_barrier((gate_g, sent))
        up_mine, gate_g = lax.optimization_barrier((up_near[0], gate_g))
        up_g = owned(up_mine, up_got)
        d_normed = finish_tokens(near_two, sent)

        def blocks_of(value):
            return value.reshape(value.shape[0], nx, nk, -1).transpose(1, 2, 0, 3)

        def rank_blocks(value):
            blocks = value.reshape(nx, nk, slice_r, row_devices, block_d)
            blocks = blocks.transpose(0, 1, 3, 2, 4)
            return blocks.reshape(nx, nk, rank, local_features)

        o_rows = after(grad_one_full, d_kv_lin)
        o_grad_t = left_trans(o_rows, attn_rows).astype(BF)
        a_o_grad_t = product(full_b_o, o_grad_t).astype(BF)
        shared = jnp.concatenate(
            [
                blocks_of(right_trans(full_a_o_t, o_grad_t)),
                blocks_of(inner(down_sides, down_all)),
                rank_blocks(
                    inner(gate_sides, gate_all) + inner(up_sides, up_all)
                ),
            ],
            axis=2,
        )
        shared = scatter_cols(shared, place_x, place_k, lambda block: block).astype(BF)
        shared = shared.reshape(3, row_devices, block_r, local_features).transpose(1, 0, 2, 3)
        o_parts = scatter_y(
            jnp.concatenate(
                [
                    o_grad_t.reshape(row_devices, block_d, q_width),
                    a_o_grad_t.reshape(row_devices, block_r, q_width),
                    shared.reshape(row_devices, 3 * block_r, local_features),
                ],
                axis=1,
            ),
            place_y,
        )
        qkv_grad = left_trans(normed, d_qkv).astype(BF)
        b_qkv_grad = left_trans(full_a_qkv, qkv_grad).astype(BF)
        a_qkv_part = rank_blocks(right_trans(full_b_qkv, qkv_grad))
        a_qkv_part = scatter_cols(a_qkv_part, place_x, place_k, lambda block: block).astype(BF)
        rank_parts = scatter_y(a_qkv_part.reshape(row_devices, block_r, local_features), place_y)
        last_parts = scatter_y(
            jnp.concatenate(
                [
                    qkv_grad.reshape(row_devices, -1, kv_width),
                    b_qkv_grad.reshape(row_devices, -1, kv_width),
                    ],
                axis=1,
            ),
            place_y,
        )
        last_parts, rank_parts, d_normed = lax.optimization_barrier(
            (last_parts, rank_parts, d_normed)
        )
        last_parts = scatter_z(last_parts, place_z)
        rank_parts = scatter_z(rank_parts, place_z)
        d_norm_one, gain_one_part = norm_backward(d_normed, own_x, gain_one, own_scale)
        grad_low_x = (d_middle + d_norm_one).astype(BF)
        o_parts = scatter_z(o_parts, place_z)
        o_parts, grad_low_x = lax.optimization_barrier((o_parts, grad_low_x))
        result_low, grad_low_x = lax.optimization_barrier((result.astype(BF), grad_low_x))
        grad_tokens = to_columns(grad_low_x).astype(F32)
        output = to_columns(result_low)
        vectors = jnp.concatenate(
            [
                gain_one_part[None],
                gain_two_part[None],
                jnp.full((1, features), square, F32),
            ],
            axis=0,
        )
        sums = sum_all(vectors)
        last_parts, rank_parts, sums = lax.optimization_barrier((last_parts, rank_parts, sums))
        down_g, d_down_side = in_place(down_g)
        gate_g, d_gate_side = in_place(gate_g)
        up_g, d_up_side = in_place(up_g)

        def join_ranks(value):
            value = value.reshape(slice_r, block_d).astype(BF)
            return jnp.concatenate(gather_cols(value, col_place), axis=0).T.astype(F32)

        rows_sum = total(o_parts)
        grad_w_o = rows_sum[:block_d].T
        grad_a_o = rows_sum[block_d:block_e].T
        grad_b_o = rows_sum[block_e : block_e + block_r]
        grad_b_down = rows_sum[block_e + block_r : block_e + 2 * block_r]
        a_gu_own = rows_sum[block_e + 2 * block_r :]
        last_sum = total(last_parts)
        wide_q = q_width + kv_width
        first_cut = block_d * wide_q // kv_width
        grad_w_qkv = last_sum[:first_cut].reshape(block_d, wide_q)
        grad_b_qkv = last_sum[first_cut:].reshape(block_r, wide_q)
        a_qkv_own = total(rank_parts)
        grad_a_gu = join_ranks(a_gu_own)
        grad_a_qkv = join_ranks(a_qkv_own)
        grad_w_q = grad_w_qkv[:, :q_width]
        grad_w_kv = grad_w_qkv[:, q_width:]
        grad_b_q = grad_b_qkv[:, :q_width]
        grad_b_kv = grad_b_qkv[:, q_width:]
        gains = lax.dynamic_slice_in_dim(sums, col_place * local_features, local_features, 1)
        loss_value = (sums[2, 0] / (2.0 * valid_count)).reshape(1)
        return (
            output,
            loss_value,
            grad_tokens,
            gains[0],
            gains[1],
            grad_w_q,
            grad_w_kv,
            grad_a_qkv,
            grad_b_q,
            grad_b_kv,
            grad_w_o,
            grad_a_o,
            grad_b_o,
            gate_g,
            up_g,
            grad_a_gu,
            d_gate_side,
            d_up_side,
            down_g.T,
            d_down_side.T,
            grad_b_down,
        )

    in_specs = (
        P("rows", "cols"),
        P("cols"),
        P("cols"),
        P("rows", "cols"),
        P("rows", "cols"),
        P("rows", None),
        P("rows", "cols"),
        P("rows", "cols"),
        P("cols", "rows"),
        P("cols", "rows"),
        P("rows", "cols"),
        P("rows", "cols"),
        P("rows", "cols"),
        P("rows", None),
        P("rows", "cols"),
        P("rows", "cols"),
        P("cols", "rows"),
        P("cols", "rows"),
        P("rows", "cols"),
        P(),
        P("rows", "cols"),
        P("rows", "cols"),
    )
    out_specs = (
        P("rows", "cols"),
        P(),
        P("rows", "cols"),
        P("cols"),
        P("cols"),
        P("rows", "cols"),
        P("rows", "cols"),
        P("rows", None),
        P("rows", "cols"),
        P("rows", "cols"),
        P("cols", "rows"),
        P("cols", "rows"),
        P("rows", "cols"),
        P("rows", "cols"),
        P("rows", "cols"),
        P("rows", None),
        P("rows", "cols"),
        P("rows", "cols"),
        P("cols", "rows"),
        P("cols", "rows"),
        P("rows", "cols"),
    )
    return jax.shard_map(shards, mesh=mesh, in_specs=in_specs, out_specs=out_specs, check_vma=False)
```
